512 devices in a mesh: group: 64 (over x, y_lo, z), member: 8 (over y_hi, core).
Axes of the slice: x: 4, y: 8 (y_hi: 4, y_lo: 2; y = y_hi * 2 + y_lo), z: 8, core: 2. Of those that a mesh axis runs over, the one named last changes fastest.
Arguments:
- load: float32 [512, 16, 768], P(('group', 'member')), may hold values from -6 to 6
- stiffness: bfloat16 [512, 768, 1024], P(('group', 'member')), as said below
- block_inverse: bfloat16 [512, 768, 1024], P(('group', 'member')), as said below
- deflation: bfloat16 [512, 32, 1024], P(('group', 'member')), may hold values from -0.375 to 0.375
- margin_rows: int32 [512, 4, 64], P(('group', 'member')), may hold values from 0 to 767
- coarse_inverse: bfloat16 [256, 64, 16384], P('member', None, 'group'), as said below
Outputs:
- solution: float32 [512, 16, 768], P(('group', 'member'))
- residual: float32 [512, 16, 768], P(('group', 'member'))
The draws below stay inside these ranges and needn't reach their ends.
Inputs may be any that keep to these rules, and one draw needn't show every extreme that they name: `margin_rows`: row numbers may repeat within a list. `stiffness`: each row's entry in the column of its own unknown (column i for row i) is the largest entry of the row in magnitude. `block_inverse`: each row's entry in the column of its own unknown is the largest entry of the row in magnitude. `coarse_inverse`: entry [l, h, j] with h * 256 + l == j is the largest entry of its row in magnitude.
All inputs are finite; a program needn't handle non-finite values.
Results may differ from the reference program's by a relative error of at most 0.0085.
Values may be sent and summed in bfloat16 or wider, within the bound.
No kernel may reach another device: no remote copies, remote signals or barrier semaphores. Data moves between devices by JAX's collectives and lax.ppermute only.
A program may use at most 64 MiB of HBM per device.

```python
from functools import partial
import jax
import jax.numpy as jnp
from jax import lax

CASES = 16
NB = 1024
QV = 64
KDEF = 32
ITERS = 2
OWNED = 768
GROUPS = 64
MEMBERS = 8
SLOTS = 512
CLOC = 256
COARSE = 16384


def dominant_rows(key, shape, diagonal_mask, noise_scale, low_end, high_end):
    noise_key, diag_key = jax.random.split(jax.random.fold_in(key, 17))
    noise = jnp.clip(jax.random.normal(noise_key, shape, jnp.float32), -5.0, 5.0) * noise_scale
    diagonal = jax.random.uniform(diag_key, shape[:-1] + (1,), jnp.float32, low_end, high_end)
    return noise + jnp.where(diagonal_mask, diagonal, 0.0)


def draw_stiffness(key, part):
    diagonal_mask = (jnp.arange(OWNED)[:, None] == jnp.arange(NB)[None, :])[None]
    values = dominant_rows(key, (SLOTS, OWNED, NB), diagonal_mask, 0.6 / NB ** 0.5, 1.0, 2.0)
    return values.astype(jnp.bfloat16)


def draw_block_inverse(key, part):
    diagonal_mask = (jnp.arange(OWNED)[:, None] == jnp.arange(NB)[None, :])[None]
    values = dominant_rows(key, (SLOTS, OWNED, NB), diagonal_mask, 0.35 / NB ** 0.5, 0.3, 0.7)
    return values.astype(jnp.bfloat16)


def draw_coarse_inverse(key, part):
    group_count = COARSE // CLOC
    row_index = jnp.arange(group_count)[None, :, None] * CLOC + jnp.arange(CLOC)[:, None, None]
    diagonal_mask = row_index == jnp.arange(COARSE)[None, None, :]
    values = dominant_rows(key, (CLOC, group_count, COARSE), diagonal_mask, 1.0 / COARSE ** 0.5, 0.3, 0.6)
    return values.astype(jnp.bfloat16)


def set_ends(drawn, rng, low, top_value):
    index_at = [jax.random.randint(jax.random.fold_in(rng, axis), (), 0, length) for axis, length in enumerate(drawn.shape)]
    longest = drawn.shape.index(max(drawn.shape))
    beside = index_at[:longest] + [(index_at[longest] + 1) % drawn.shape[longest]] + index_at[longest + 1:]
    return drawn.at[tuple(index_at)].set(low).at[tuple(beside)].set(top_value)


def block_levels(stream_key, dims, cuts, least, top_value):
    def one(position, blocks):
        heights = jax.random.uniform(jax.random.fold_in(jax.random.fold_in(stream_key, 6), position), (blocks,), jnp.float32, least / len(cuts), top_value / len(cuts))
        return jnp.repeat(jnp.exp(heights), dims[position] // blocks).reshape((-1,) + (1,) * (len(dims) - position - 1))

    factor_of = one(*cuts[0])
    for cut in cuts[1:]:
        factor_of = factor_of * one(*cut)
    return factor_of


def gaussian(rng, shape, width, bound, shards=(), held_as=jnp.bfloat16):
    drawn = width * jax.random.normal(rng, shape, jnp.float32)
    if shards:
        drawn = drawn * block_levels(rng, shape, shards, -0.22, 0.18)
    return jnp.clip(drawn, -bound, bound).astype(held_as)


def setup_inputs(seed: int = 0) -> dict:
    key_of = jax.random.split(jax.random.key(seed), 7)
    load = gaussian(key_of[0], (SLOTS, CASES, OWNED), 1.0, 6.0, ((0, 512),), jnp.float32)
    stiffness = draw_stiffness(jax.random.fold_in(key_of[6], 71), 0)
    block_inverse = draw_block_inverse(jax.random.fold_in(key_of[6], 71), 0)
    deflation = gaussian(key_of[3], (SLOTS, KDEF, NB), (8 * KDEF) ** -0.5, 0.375, ((0, 512),))
    margin_rows = set_ends(jax.random.randint(key_of[4], (SLOTS, 4, QV), 0, OWNED), jax.random.fold_in(key_of[4], 1), 0, OWNED - 1).astype(jnp.int32)
    coarse_inverse = draw_coarse_inverse(jax.random.fold_in(key_of[6], 71), 0)
    return {"load": load, "stiffness": stiffness, "block_inverse": block_inverse, "deflation": deflation, "margin_rows": margin_rows, "coarse_inverse": coarse_inverse}


def neighbour_slots():
    slot_ids = jnp.arange(SLOTS, dtype=jnp.int32)
    group_ids = slot_ids // MEMBERS
    member_ids = slot_ids % MEMBERS
    return jnp.stack([((group_ids - 1) % GROUPS) * MEMBERS + member_ids,
                      ((group_ids + 1) % GROUPS) * MEMBERS + member_ids,
                      group_ids * MEMBERS + (member_ids - 1) % MEMBERS,
                      group_ids * MEMBERS + (member_ids + 1) % MEMBERS], axis=1).astype(jnp.int32)


def extend(values, margin_rows, neighbours):
    def one_block(slot_index):
        pieces = [values[slot_index]]
        for direction in range(4):
            source = values[neighbours[slot_index, direction]]
            pieces.append(jnp.take(source, margin_rows[slot_index, direction], axis=1))
        return jnp.concatenate(pieces, axis=1)
    return lax.map(one_block, jnp.arange(SLOTS, dtype=jnp.int32))


def project_rows(operands):
    left_side, matrix_rows = operands
    return jnp.dot(left_side, matrix_rows.T, preferred_element_type=jnp.float32)


def group_product(vector_rows, group_slab):
    return jnp.dot(vector_rows, group_slab.T, preferred_element_type=jnp.float32)


def fine_correction(operands):
    block_values, inverse_rows, prolong_rows, basis_rows = operands
    local_part = jnp.dot(block_values, inverse_rows.T, preferred_element_type=jnp.float32)
    return local_part + jnp.dot(prolong_rows, basis_rows[:, :OWNED], preferred_element_type=jnp.float32)


def reference(load, stiffness, block_inverse, deflation, margin_rows, coarse_inverse):
    neighbours = neighbour_slots()
    residual = load
    solution = jnp.zeros_like(residual)
    columns_first = jnp.transpose(coarse_inverse, (1, 0, 2))
    for step_index in range(ITERS):
        block_values = extend(residual.astype(jnp.bfloat16), margin_rows, neighbours)
        coefficients = lax.map(project_rows, (block_values, deflation)).astype(jnp.bfloat16)
        grouped = coefficients.reshape(GROUPS, MEMBERS, CASES, KDEF)
        coarse_vector = jnp.transpose(grouped, (2, 0, 1, 3)).reshape(CASES, COARSE)
        coarse_result = lax.map(partial(group_product, coarse_vector), columns_first)
        prolong = jnp.transpose(coarse_result.reshape(GROUPS, CASES, MEMBERS, KDEF), (0, 2, 1, 3))
        prolong = prolong.reshape(SLOTS, CASES, KDEF).astype(jnp.bfloat16)
        correction = lax.map(fine_correction, (block_values, block_inverse, prolong, deflation))
        solution = solution + correction
        solution_block = extend(solution.astype(jnp.bfloat16), margin_rows, neighbours)
        residual = load - lax.map(project_rows, (solution_block, stiffness))
    return solution, residual
```

```python
import jax
import jax.numpy as jnp
from jax import lax
from jax.sharding import PartitionSpec as P

ITERS = 2


def from_behind(shard, axis, by):
    peers = lax.axis_size(axis)
    return lax.ppermute(shard, axis, [(i, (i + by) % peers) for i in range(peers)])


def local(load, stiffness, block_inverse, deflation, margin_rows, coarse_inverse):
    own_load = load[0]
    stiff_rows = stiffness[0]
    inverse_rows = block_inverse[0]
    basis_rows = deflation[0]
    own_lists = margin_rows[0]
    owned_count = own_load.shape[1]

    def extend(values):
        from_group_lower = from_behind(values, "group", 1)
        from_group_upper = from_behind(values, "group", -1)
        from_member_lower = from_behind(values, "member", 1)
        from_member_upper = from_behind(values, "member", -1)
        pieces = [
            jnp.take(from_group_lower, own_lists[0], axis=1),
            jnp.take(from_group_upper, own_lists[1], axis=1),
            jnp.take(from_member_lower, own_lists[2], axis=1),
            jnp.take(from_member_upper, own_lists[3], axis=1),
        ]
        return jnp.concatenate([values] + pieces, axis=1)

    solution = jnp.zeros_like(own_load)
    residual = own_load
    for step_index in range(ITERS):
        block_values = extend(residual.astype(jnp.bfloat16))
        own_coef = jnp.einsum(
            "cn,kn->ck", block_values, basis_rows, preferred_element_type=jnp.float32
        ).astype(jnp.bfloat16)
        gathered = lax.all_gather(own_coef, "member", axis=1, tiled=True)
        shares = jnp.einsum("lhj,cj->hcl", coarse_inverse, gathered, preferred_element_type=jnp.float32)
        arrived = lax.all_to_all(shares, "group", 0, 0, tiled=True)
        prolong = jnp.sum(arrived, axis=0).astype(jnp.bfloat16)
        local_fix = jnp.einsum(
            "cn,un->cu", block_values, inverse_rows, preferred_element_type=jnp.float32
        )
        correction = local_fix + jnp.dot(
            prolong, basis_rows[:, :owned_count], preferred_element_type=jnp.float32
        )
        solution = solution + correction
        solution_block = extend(solution.astype(jnp.bfloat16))
        applied = jnp.einsum(
            "cn,un->cu", solution_block, stiff_rows, preferred_element_type=jnp.float32
        )
        residual = own_load - applied
    return (solution[None], residual[None])


def solution(mesh):
    placed = (
        P(("group", "member"), None, None),
        P(("group", "member"), None, None),
        P(("group", "member"), None, None),
        P(("group", "member"), None, None),
        P(("group", "member"), None, None),
        P("member", None, "group"),
    )
    return jax.shard_map(
        local,
        mesh=mesh,
        in_specs=placed,
        out_specs=(P(("group", "member"), None, None), P(("group", "member"), None, None)),
        check_vma=False,
    )
```

```python
import jax
import jax.numpy as jnp
from jax import lax
from jax.experimental import pallas as pl
from jax.experimental.pallas import tpu as pltpu
from jax.sharding import PartitionSpec as P

ITERS = 2
LANES = 128
F32 = jnp.float32
BF16 = jnp.bfloat16
VMEM = pltpu.VMEM


def from_behind(shard, axis, by):
    peers = lax.axis_size(axis)
    return lax.ppermute(shard, axis, [(i, (i + by) % peers) for i in range(peers)])


def call(body, outs, *args):
    return pl.pallas_call(
        body,
        out_shape=[jax.ShapeDtypeStruct(shape, dtype) for shape, dtype in outs],
        in_specs=[pl.BlockSpec(memory_space=VMEM)] * len(args),
        out_specs=[pl.BlockSpec(memory_space=VMEM)] * len(outs),
        compiler_params=pltpu.CompilerParams(vmem_limit_bytes=16 * 2**20),
    )(*args)


def dot_nt(left, right):
    return lax.dot_general(left, right, (((1,), (1,)), ((), ())), preferred_element_type=F32)


def dot_nn(left, right):
    return jnp.dot(left, right, preferred_element_type=F32)


def margins(fields, picks):
    cases = fields[0].shape[0]
    width = picks.shape[1] // len(fields)
    every = dot_nn(jnp.concatenate(fields, axis=0), picks)
    owner = lax.broadcasted_iota(jnp.int32, (cases, picks.shape[1]), 1) // width
    kept = every[:cases]
    for d in range(1, len(fields)):
        kept = jnp.where(owner == d, every[d * cases : (d + 1) * cases], kept)
    return kept.astype(BF16)


def restrict_body(v, f0, f1, f2, f3, picks, basis, block, coef):
    edge = margins([f0[...], f1[...], f2[...], f3[...]], picks[...])
    whole = jnp.concatenate([v[...], edge], axis=1)
    block[...] = whole
    tall = jnp.concatenate([whole] * (LANES // whole.shape[0]), axis=0)
    part = dot_nt(basis[...], tall).astype(BF16)
    for m in range(coef.shape[0]):
        coef[m] = part


def coarse_body(coef, inverse, share):
    peers, kdef, _ = coef.shape
    cases = 16
    per = LANES // cases
    every = coef[...].reshape(peers * kdef, LANES)
    lane = lax.broadcasted_iota(jnp.int32, every.shape, 1) // cases
    tiles = inverse.shape[0] // per
    sums = [None] * tiles
    for q in range(per):
        here = jnp.where(lane == q, every, jnp.zeros_like(every))
        for t in range(tiles):
            term = dot_nn(inverse[per * t + q], here)
            sums[t] = term if sums[t] is None else sums[t] + term
    for t in range(tiles):
        share[:, t, :] = sums[t]


def prolong_of(arrived, kdef):
    cases = 16
    total = jnp.sum(arrived, axis=0)
    tiles = total.shape[0]
    row = lax.broadcasted_iota(jnp.int32, (cases, LANES), 0)
    lane = lax.broadcasted_iota(jnp.int32, (cases, LANES), 1)
    out = None
    for t in range(tiles):
        spread = jnp.where(lane % cases == row, total[t : t + 1], 0.0).astype(BF16)
        target = lax.broadcasted_iota(jnp.int32, (LANES, kdef), 0) // cases + t * (LANES // cases)
        onto = (target == lax.broadcasted_iota(jnp.int32, (LANES, kdef), 1)).astype(BF16)
        term = dot_nn(spread, onto)
        out = term if out is None else out + term
    return out.astype(BF16)


def correct_body(first, arrived, block, inverse, basis, *rest):
    if first:
        total, rounded = rest
    else:
        before, total, rounded = rest
    owned = total.shape[1]
    value = dot_nt(block[...], inverse[...])
    prolong = prolong_of(arrived[...], basis.shape[0])
    value = value + dot_nn(prolong, basis[:, :owned])
    if not first:
        value = before[...] + value
    total[...] = value
    rounded[...] = value.astype(BF16)


def residual_body(last, v, f0, f1, f2, f3, picks, stiff, load, *outs):
    edge = margins([f0[...], f1[...], f2[...], f3[...]], picks[...])
    whole = jnp.concatenate([v[...], edge], axis=1)
    value = load[...] - dot_nt(whole, stiff[...])
    outs[0][...] = value if last else value.astype(BF16)


def local(load, stiffness, block_inverse, deflation, margin_rows, coarse_inverse):
    own_load = load[0]
    stiff_rows = stiffness[0]
    inverse_rows = block_inverse[0]
    basis_rows = deflation[0]
    cases, owned = own_load.shape
    kdef, nb = basis_rows.shape
    groups = lax.axis_size("group")
    members = lax.axis_size("member")
    tiles = coarse_inverse.shape[0] * cases // LANES
    picks = (
        lax.broadcasted_iota(jnp.int32, (owned, nb - owned), 0) == margin_rows[0].reshape(1, nb - owned)
    ).astype(BF16)

    def around(values):
        return (
            from_behind(values, "group", 1),
            from_behind(values, "group", -1),
            from_behind(values, "member", 1),
            from_behind(values, "member", -1),
        )

    field = own_load.astype(BF16)
    solution = None
    for step in range(ITERS):
        block, coef = call(
            restrict_body,
            [((cases, nb), BF16), ((members, kdef, LANES), BF16)],
            field, *around(field), picks, basis_rows,
        )
        gathered = lax.all_to_all(coef, "member", 0, 0, tiled=True)
        (share,) = call(coarse_body, [((groups, tiles, LANES), F32)], gathered, coarse_inverse)
        arrived = lax.all_to_all(share, "group", 0, 0, tiled=True)
        before = () if step == 0 else (solution,)
        solution, rounded = call(
            lambda *refs: correct_body(step == 0, *refs),
            [((cases, owned), F32), ((cases, owned), BF16)],
            arrived, block, inverse_rows, basis_rows, *before,
        )
        last = step == ITERS - 1
        (field,) = call(
            lambda *refs: residual_body(last, *refs),
            [((cases, owned), F32 if last else BF16)],
            rounded, *around(rounded), picks, stiff_rows, own_load,
        )
    return (solution[None], field[None])


def solution(mesh):
    placed = (
        P(("group", "member"), None, None),
        P(("group", "member"), None, None),
        P(("group", "member"), None, None),
        P(("group", "member"), None, None),
        P(("group", "member"), None, None),
        P("member", None, "group"),
    )
    return jax.shard_map(
        local,
        mesh=mesh,
        in_specs=placed,
        out_specs=(P(("group", "member"), None, None), P(("group", "member"), None, None)),
        check_vma=False,
    )
```

```python
import jax
import jax.numpy as jnp
from jax import lax
from jax.experimental import pallas as pl
from jax.experimental.pallas import tpu as pltpu
from jax.sharding import PartitionSpec as P

ITERS = 2
LANES = 128
F32 = jnp.float32
BF16 = jnp.bfloat16
VMEM = pltpu.VMEM


def from_behind(shard, axis, by):
    peers = lax.axis_size(axis)
    return lax.ppermute(shard, axis, [(i, (i + by) % peers) for i in range(peers)])


def call(body, outs, *args):
    return pl.pallas_call(
        body,
        out_shape=[jax.ShapeDtypeStruct(shape, dtype) for shape, dtype in outs],
        in_specs=[pl.BlockSpec(memory_space=VMEM)] * len(args),
        out_specs=[pl.BlockSpec(memory_space=VMEM)] * len(outs),
        compiler_params=pltpu.CompilerParams(vmem_limit_bytes=16 * 2**20),
    )(*args)


def dot_nt(left, right):
    return lax.dot_general(left, right, (((1,), (1,)), ((), ())), preferred_element_type=F32)


def dot_nn(left, right):
    return jnp.dot(left, right, preferred_element_type=F32)


def exchanged(shard, axis, first):
    peers = lax.axis_size(axis)
    pairs = [((first + i) % peers, (first + (i ^ 1)) % peers) for i in range(peers)]
    return lax.ppermute(shard, axis, pairs)


def margins(fields, picks, owner):
    cases = fields[0].shape[0]
    every = dot_nn(jnp.concatenate(fields, axis=0), picks)
    kept = every[:cases]
    for d in range(1, len(fields)):
        kept = jnp.where(owner == d, every[d * cases : (d + 1) * cases], kept)
    return kept.astype(BF16)


def restrict_body(v, pair, other, lower, upper, picks, owner, basis, block, coef):
    edge = margins([lower[...], upper[...], pair[...], other[...]], picks[...], owner[...])
    whole = jnp.concatenate([v[...], edge], axis=1)
    block[...] = whole
    tall = jnp.concatenate([whole] * (LANES // whole.shape[0]), axis=0)
    part = dot_nt(basis[...], tall).astype(BF16)
    for m in range(coef.shape[0]):
        coef[m] = part


def coarse_body(coef, inverse, share):
    peers, kdef, _ = coef.shape
    cases = 16
    per = LANES // cases
    every = coef[...].reshape(peers * kdef, LANES)
    lane = lax.broadcasted_iota(jnp.int32, every.shape, 1) // cases
    tiles = inverse.shape[0] // per
    sums = [None] * tiles
    for q in range(per):
        here = jnp.where(lane == q, every, jnp.zeros_like(every))
        for t in range(tiles):
            term = dot_nn(inverse[per * t + q], here)
            sums[t] = term if sums[t] is None else sums[t] + term
    for t in range(tiles):
        share[:, t, :] = sums[t]


def prolong_of(arrived, kdef):
    cases = 16
    total = jnp.sum(arrived, axis=0)
    tiles = total.shape[0]
    row = lax.broadcasted_iota(jnp.int32, (cases, LANES), 0)
    lane = lax.broadcasted_iota(jnp.int32, (cases, LANES), 1)
    out = None
    for t in range(tiles):
        spread = jnp.where(lane % cases == row, total[t : t + 1], 0.0).astype(BF16)
        target = lax.broadcasted_iota(jnp.int32, (LANES, kdef), 0) // cases + t * (LANES // cases)
        onto = (target == lax.broadcasted_iota(jnp.int32, (LANES, kdef), 1)).astype(BF16)
        term = dot_nn(spread, onto)
        out = term if out is None else out + term
    return out.astype(BF16)


def correct_body(first, arrived, block, inverse, basis, *rest):
    if first:
        total, rounded = rest
    else:
        before, total, rounded = rest
    owned = total.shape[1]
    value = dot_nt(block[...], inverse[...])
    prolong = prolong_of(arrived[...], basis.shape[0])
    value = value + dot_nn(prolong, basis[:, :owned])
    if not first:
        value = before[...] + value
    total[...] = value
    rounded[...] = value.astype(BF16)


def residual_body(last, v, pair, other, lower, upper, picks, owner, stiff, load, *rest):
    edge = margins([lower[...], upper[...], pair[...], other[...]], picks[...], owner[...])
    whole = jnp.concatenate([v[...], edge], axis=1)
    value = load[...] - dot_nt(whole, stiff[...])
    if last:
        total, out, passed = rest
        passed[...] = total[...]
        out[...] = value
    else:
        rest[0][...] = value.astype(BF16)


def local(load, stiffness, block_inverse, deflation, margin_rows, coarse_inverse):
    own_load = load[0]
    stiff_rows = stiffness[0]
    inverse_rows = block_inverse[0]
    basis_rows = deflation[0]
    cases, owned = own_load.shape
    kdef, nb = basis_rows.shape
    groups = lax.axis_size("group")
    members = lax.axis_size("member")
    tiles = coarse_inverse.shape[0] * cases // LANES
    picks = (
        lax.broadcasted_iota(jnp.int32, (owned, nb - owned), 0) == margin_rows[0].reshape(1, nb - owned)
    ).astype(BF16)

    source = lax.broadcasted_iota(jnp.int32, (1, nb - owned), 1) // margin_rows.shape[2]
    even = lax.axis_index("member") % 2 == 0
    owner = jnp.where((source >= 2) & even, 5 - source, source)

    def around(values):
        from_pair = exchanged(values, "member", 0)
        from_other = exchanged(values, "member", 1)
        from_lower = from_behind(values, "group", 1)
        from_upper = from_behind(values, "group", -1)
        return from_pair, from_other, from_lower, from_upper

    field = own_load.astype(BF16)
    solution = None
    for step in range(ITERS):
        block, coef = call(
            restrict_body,
            [((cases, nb), BF16), ((members, kdef, LANES), BF16)],
            field, *around(field), picks, owner, basis_rows,
        )
        gathered = lax.all_to_all(coef, "member", 0, 0, tiled=True)
        (share,) = call(coarse_body, [((groups, tiles, LANES), F32)], gathered, coarse_inverse)
        arrived = lax.all_to_all(share, "group", 0, 0, tiled=True)
        before = () if step == 0 else (solution,)
        solution, rounded = call(
            lambda *refs: correct_body(step == 0, *refs),
            [((cases, owned), F32), ((cases, owned), BF16)],
            arrived, block, inverse_rows, basis_rows, *before,
        )
        last = step == ITERS - 1
        kept = (solution,) if last else ()
        field, *passed = call(
            lambda *refs: residual_body(last, *refs),
            [((cases, owned), F32 if last else BF16)] + [((cases, owned), F32)] * last,
            rounded, *around(rounded), picks, owner, stiff_rows, own_load, *kept,
        )
    return (passed[0][None], field[None])


def solution(mesh):
    placed = (
        P(("group", "member"), None, None),
        P(("group", "member"), None, None),
        P(("group", "member"), None, None),
        P(("group", "member"), None, None),
        P(("group", "member"), None, None),
        P("member", None, "group"),
    )
    return jax.shard_map(
        local,
        mesh=mesh,
        in_specs=placed,
        out_specs=(P(("group", "member"), None, None), P(("group", "member"), None, None)),
        check_vma=False,
    )
```

```python
import jax
import jax.numpy as jnp
from jax import lax
from jax.experimental import pallas as pl
from jax.experimental.pallas import tpu as pltpu
from jax.sharding import PartitionSpec as P

ITERS = 2
LANES = 128
HALF = 64
CASES = 16
DIGIT = 32
F32 = jnp.float32
BF16 = jnp.bfloat16
VMEM = pltpu.VMEM


def from_behind(shard, axis, by):
    peers = lax.axis_size(axis)
    return lax.ppermute(shard, axis, [(i, (i + by) % peers) for i in range(peers)])


def exchanged(shard, axis, first):
    peers = lax.axis_size(axis)
    pairs = [((first + i) % peers, (first + (i ^ 1)) % peers) for i in range(peers)]
    return lax.ppermute(shard, axis, pairs)


def call(body, outs, *args):
    return pl.pallas_call(
        body,
        out_shape=[jax.ShapeDtypeStruct(shape, dtype) for shape, dtype in outs],
        in_specs=[pl.BlockSpec(memory_space=VMEM)] * len(args),
        out_specs=[pl.BlockSpec(memory_space=VMEM)] * len(outs),
        compiler_params=pltpu.CompilerParams(vmem_limit_bytes=16 * 2**20),
        cost_estimate=pl.CostEstimate(flops=2**24, bytes_accessed=2**19, transcendentals=0),
    )(*args)


def dot_nt(left, right):
    return lax.dot_general(left, right, (((1,), (1,)), ((), ())), preferred_element_type=F32)


def dot_nn(left, right):
    return jnp.dot(left, right, preferred_element_type=F32)


def even_member():
    return lax.rem(lax.axis_index("member"), 2) == 0


def tall(rows):
    return jnp.concatenate([rows] * (LANES // rows.shape[0]), axis=0)


def lanes(shape):
    return lax.broadcasted_iota(jnp.int32, shape, 1)


def margins(lower, upper, pair, other, picks):
    every = dot_nn(jnp.concatenate([lower, upper, pair, other], axis=0), picks)
    source = lanes((CASES, picks.shape[1])) // HALF
    owner = jnp.where((source >= 2) & even_member(), 5 - source, source)
    kept = every[:CASES]
    for d in range(1, 4):
        kept = jnp.where(owner == d, every[d * CASES : (d + 1) * CASES], kept)
    return kept.astype(BF16)


def prepare_body(rows, basis, picks, held, for_pair, for_other):
    lists = rows[0]
    nb = basis.shape[1]
    owned = picks.shape[0]
    flat = jnp.concatenate([lists[d : d + 1] for d in range(4)], axis=1)
    spots = lax.broadcasted_iota(jnp.int32, picks.shape, 0)
    picks[...] = jnp.where(spots == flat, 1.0, 0.0).astype(BF16)
    held[...] = basis[...]
    even = even_member()
    edge = basis[:, nb - LANES :].astype(F32)
    edge = jnp.where(even, edge, pltpu.roll(edge, HALF, 1))
    turn = jnp.where(even, flat[:, LANES:], jnp.concatenate([lists[3:4], lists[2:3]], axis=1))
    high = jnp.broadcast_to((turn // DIGIT).astype(F32), edge.shape)
    low = jnp.broadcast_to((turn % DIGIT).astype(F32), edge.shape)
    parts = jnp.concatenate([edge, high, low], axis=1)
    side = lanes(parts.shape) % LANES >= HALF
    half = parts.shape[0] // 2
    for out, mine in ((for_pair, side), (for_other, jnp.logical_not(side))):
        kept = jnp.where(mine, parts, 0.0).astype(BF16)
        out[...] = jnp.concatenate([kept[:half], kept[half:]], axis=1)


def restrict_body(v, pair, other, lower, upper, picks, basis, block, coef):
    edge = margins(lower[...], upper[...], pair[...], other[...], picks[...])
    whole = jnp.concatenate([v[...], edge], axis=1)
    block[...] = whole
    part = dot_nt(basis[...], tall(whole)).astype(BF16)
    for m in range(coef.shape[0]):
        coef[m] = part


def mixed_body(v, lower, upper, pair, other, picks, basis, edge, message):
    value = v[...]
    rows = jnp.concatenate([lower[...], upper[...]], axis=0)
    every = dot_nn(rows, picks[:, :LANES])
    lane = lanes((CASES, LANES))
    near = jnp.where(lane < HALF, every[:CASES], every[CASES:]).astype(BF16)
    edge[...] = near
    known = jnp.concatenate([value, near], axis=1)
    own = dot_nt(basis[:, : known.shape[1]], tall(known))
    width = 3 * LANES
    unfold = lambda ref: jnp.concatenate([ref[CASES:, :width], ref[CASES:, width:]], axis=0)
    first, second = unfold(pair), unfold(other)
    digits = (first[:1, LANES:] + second[:1, LANES:]).astype(F32)
    spot = (digits[:, :LANES] * DIGIT + digits[:, LANES:]).astype(jnp.int32)
    choice = lax.broadcasted_iota(jnp.int32, (value.shape[1], LANES), 0) == spot
    chosen = dot_nn(value, jnp.where(choice, 1.0, 0.0).astype(BF16))
    spread = tall(chosen.astype(BF16))
    to_first = dot_nt(first[:, :LANES], spread)
    to_second = dot_nt(second[:, :LANES], spread)
    head = own.astype(BF16).astype(F32)
    place = lanes(own.shape) // CASES
    out = jnp.concatenate([chosen, pltpu.roll(chosen, HALF, 1)], axis=0)
    out = jnp.where(place == 3, to_second, out)
    out = jnp.where(place == 2, to_first, out)
    out = jnp.where(place == 1, own - head, out)
    out = jnp.where(place == 0, head, out).astype(BF16)
    for m in range(message.shape[0]):
        message[m] = out


def shares_of(every, inverse, share):
    per = LANES // CASES
    lane = lanes(every.shape) // CASES
    tiles = inverse.shape[0] // per
    sums = [None] * tiles
    for q in range(per):
        here = jnp.where(lane == q, every, jnp.zeros_like(every))
        for t in range(tiles):
            term = dot_nn(inverse[per * t + q], here)
            sums[t] = term if sums[t] is None else sums[t] + term
    for t in range(tiles):
        share[:, t, :] = sums[t]


def coarse_body(coef, inverse, share):
    shares_of(coef[...].reshape(-1, LANES), inverse, share)


def coarse_mixed_body(message, inverse, share):
    peers, kdef, _ = message.shape
    source = lax.broadcasted_iota(jnp.int32, (LANES, 3 * LANES), 0)
    target = lanes((LANES, 3 * LANES))
    group = source // CASES
    part = jnp.where(group < 2, 0, group - 1)
    hit = (part == target // LANES) & (source % CASES == target % CASES)
    parts = dot_nn(message[...].reshape(peers * kdef, LANES), jnp.where(hit, 1.0, 0.0).astype(BF16))
    every = []
    for m in range(peers):
        pair = m ^ 1
        other = (m + 1) % peers if m % 2 else (m - 1) % peers
        at = lambda k, j: parts[k * kdef : (k + 1) * kdef, j * LANES : (j + 1) * LANES]
        every.append(at(m, 0) + at(pair, 1) + at(other, 2))
    shares_of(jnp.concatenate(every, axis=0).astype(BF16), inverse, share)


def prolong_of(arrived, kdef):
    total = jnp.sum(arrived, axis=0)
    tiles = total.shape[0]
    row = lax.broadcasted_iota(jnp.int32, (CASES, LANES), 0)
    lane = lanes((CASES, LANES))
    out = None
    for t in range(tiles):
        spread = jnp.where(lane % CASES == row, total[t : t + 1], 0.0).astype(BF16)
        target = lax.broadcasted_iota(jnp.int32, (LANES, kdef), 0) // CASES + t * (LANES // CASES)
        onto = (target == lanes((LANES, kdef))).astype(BF16)
        term = dot_nn(spread, onto)
        out = term if out is None else out + term
    return out.astype(BF16)


def correct_body(arrived, block, inverse, basis, for_pair, for_other, total, rounded, pair, other):
    value = dot_nt(block[...], inverse[...])
    prolong = prolong_of(arrived[...], basis.shape[0])
    value = value + dot_nn(prolong, basis[:, : total.shape[1]])
    total[...] = value
    short = value.astype(BF16)
    rounded[...] = short
    for out, more in ((pair, for_pair), (other, for_other)):
        out[:CASES] = short
        out[CASES:] = more[...]


def correct_mixed_body(arrived, v, edge, message, inverse, basis, before, total, rounded):
    me = lax.axis_index("member")
    peers = message.shape[0]
    even = even_member()
    pair = jnp.where(even, me + 1, me - 1)
    other = lax.rem(jnp.where(even, me + peers - 1, me + 1), peers)
    from_pair = message[pair, :CASES].astype(F32)
    from_other = message[other, CASES:].astype(F32)
    high = jnp.where(even, from_pair, from_other)
    low = jnp.where(even, from_other, from_pair)
    far = jnp.where(lanes(high.shape) < HALF, pltpu.roll(low, HALF, 1), high).astype(BF16)
    block = jnp.concatenate([v[...], edge[...], far], axis=1)
    value = dot_nt(block, inverse[...])
    prolong = prolong_of(arrived[...], basis.shape[0])
    value = before[...] + (value + dot_nn(prolong, basis[:, : total.shape[1]]))
    total[...] = value
    rounded[...] = value.astype(BF16)


def residual_body(last, v, pair, other, lower, upper, picks, stiff, load, *rest):
    edge = margins(lower[...], upper[...], pair[:CASES], other[:CASES], picks[...])
    whole = jnp.concatenate([v[...], edge], axis=1)
    value = load[...] - dot_nt(whole, stiff[...])
    if last:
        total, out, passed = rest
        passed[...] = total[...]
        out[...] = value
    else:
        rest[0][...] = value.astype(BF16)


def local(load, stiffness, block_inverse, deflation, margin_rows, coarse_inverse):
    own_load = load[0]
    stiff_rows = stiffness[0]
    inverse_rows = block_inverse[0]
    cases, owned = own_load.shape
    kdef, nb = deflation.shape[1:]
    groups = lax.axis_size("group")
    members = lax.axis_size("member")
    tiles = coarse_inverse.shape[0] * cases // LANES

    def group_around(values):
        return from_behind(values, "group", 1), from_behind(values, "group", -1)

    def member_around(for_pair, for_other):
        return exchanged(for_pair, "member", 0), exchanged(for_other, "member", 1)

    field = own_load.astype(BF16)
    near = member_around(field, field)
    far = group_around(field)
    picks, basis, for_pair, for_other = call(
        prepare_body,
        [((owned, nb - owned), BF16), ((kdef, nb), BF16)] + [((kdef // 2, 6 * LANES), BF16)] * 2,
        margin_rows, deflation[0],
    )
    block, coef = call(
        restrict_body,
        [((cases, nb), BF16), ((members, kdef, LANES), BF16)],
        field, *near, *far, picks, basis,
    )
    gathered = lax.all_to_all(coef, "member", 0, 0, tiled=True)
    share_shape = [((groups, tiles, LANES), F32)]
    (share,) = call(coarse_body, share_shape, gathered, coarse_inverse)
    arrived = lax.all_to_all(share, "group", 0, 0, tiled=True)
    total, rounded, for_pair, for_other = call(
        correct_body,
        [((cases, owned), F32), ((cases, owned), BF16)] + [((cases + kdef // 2, owned), BF16)] * 2,
        arrived, block, inverse_rows, basis, for_pair, for_other,
    )
    near = member_around(for_pair, for_other)
    (field,) = call(
        lambda *refs: residual_body(False, *refs),
        [((cases, owned), BF16)],
        rounded, *near, *group_around(rounded), picks, stiff_rows, own_load,
    )

    edge, message = call(
        mixed_body,
        [((cases, LANES), BF16), ((members, kdef, LANES), BF16)],
        field, *group_around(field), *near, picks, basis,
    )
    message = lax.all_to_all(message, "member", 0, 0, tiled=True)
    (share,) = call(coarse_mixed_body, share_shape, message, coarse_inverse)
    arrived = lax.all_to_all(share, "group", 0, 0, tiled=True)
    total, rounded = call(
        correct_mixed_body,
        [((cases, owned), F32), ((cases, owned), BF16)],
        arrived, field, edge, message, inverse_rows, basis, total,
    )
    residual, solution_out = call(
        lambda *refs: residual_body(True, *refs),
        [((cases, owned), F32)] * 2,
        rounded, *member_around(rounded, rounded), *group_around(rounded), picks, stiff_rows, own_load, total,
    )
    return (solution_out[None], residual[None])


def solution(mesh):
    placed = (
        P(("group", "member"), None, None),
        P(("group", "member"), None, None),
        P(("group", "member"), None, None),
        P(("group", "member"), None, None),
        P(("group", "member"), None, None),
        P("member", None, "group"),
    )
    return jax.shard_map(
        local,
        mesh=mesh,
        in_specs=placed,
        out_specs=(P(("group", "member"), None, None), P(("group", "member"), None, None)),
        check_vma=False,
    )
```

```python
import jax
import jax.numpy as jnp
from jax import lax
from jax.experimental import pallas as pl
from jax.experimental.pallas import tpu as pltpu
from jax.sharding import PartitionSpec as P


LANES = 128
HALF = 64
CASES = 16
DIGIT = 32
F32 = jnp.float32
BF16 = jnp.bfloat16
VMEM = pltpu.VMEM


def from_behind(shard, axis, by):
    peers = lax.axis_size(axis)
    return lax.ppermute(shard, axis, [(i, (i + by) % peers) for i in range(peers)])


def exchanged(shard, axis, first):
    peers = lax.axis_size(axis)
    pairs = [((first + i) % peers, (first + (i ^ 1)) % peers) for i in range(peers)]
    return lax.ppermute(shard, axis, pairs)


def call(body, outs, *args, space=VMEM, scratch=()):
    return pl.pallas_call(
        body,
        out_shape=[jax.ShapeDtypeStruct(shape, dtype) for shape, dtype in outs],
        in_specs=[pl.BlockSpec(memory_space=space)] * len(args),
        out_specs=[pl.BlockSpec(memory_space=VMEM)] * len(outs),
        scratch_shapes=list(scratch),
        compiler_params=pltpu.CompilerParams(vmem_limit_bytes=16 * 2**20),
    )(*args)


def dot_nt(left, right):
    return lax.dot_general(left, right, (((1,), (1,)), ((), ())), preferred_element_type=F32)


def dot_nn(left, right):
    return jnp.dot(left, right, preferred_element_type=F32)


def even_member():
    return lax.rem(lax.axis_index("member"), 2) == 0


def tall(rows):
    return jnp.concatenate([rows] * (LANES // rows.shape[0]), axis=0)


def lanes(shape):
    return lax.broadcasted_iota(jnp.int32, shape, 1)


def margins(lower, upper, pair, other, picks):
    every = dot_nn(jnp.concatenate([lower, upper, pair, other], axis=0), picks)
    source = lanes((CASES, picks.shape[1])) // HALF
    owner = jnp.where((source >= 2) & even_member(), 5 - source, source)
    kept = every[:CASES]
    for d in range(1, 4):
        kept = jnp.where(owner == d, every[d * CASES : (d + 1) * CASES], kept)
    return kept.astype(BF16)


def begin_body(far_load, far_rows, far_basis, far_inverse, field, picks, basis, for_pair, for_other, inverse,
               load, rows, sems):
    moves = [
        pltpu.make_async_copy(source, target, sems.at[i])
        for i, (source, target) in enumerate(
            ((far_load, load), (far_rows, rows), (far_basis, basis), (far_inverse, inverse))
        )
    ]
    for move in moves:
        move.start()
    moves[1].wait()
    lists = rows[0]
    nb = basis.shape[1]
    flat = jnp.concatenate([lists[d : d + 1] for d in range(4)], axis=1)
    spots = lax.broadcasted_iota(jnp.int32, picks.shape, 0)
    picks[...] = jnp.where(spots == flat, 1.0, 0.0).astype(BF16)
    moves[0].wait()
    field[...] = load[...].astype(BF16)
    moves[2].wait()
    even = even_member()
    edge = basis[:, nb - LANES :].astype(F32)
    edge = jnp.where(even, edge, pltpu.roll(edge, HALF, 1))
    turn = jnp.where(even, flat[:, LANES:], jnp.concatenate([lists[3:4], lists[2:3]], axis=1))
    high = jnp.broadcast_to((turn // DIGIT).astype(F32), edge.shape)
    low = jnp.broadcast_to((turn % DIGIT).astype(F32), edge.shape)
    parts = jnp.concatenate([edge, high, low], axis=1)
    side = lanes(parts.shape) % LANES >= HALF
    half = parts.shape[0] // 2
    for out, mine in ((for_pair, side), (for_other, jnp.logical_not(side))):
        kept = jnp.where(mine, parts, 0.0).astype(BF16)
        out[...] = jnp.concatenate([kept[:half], kept[half:]], axis=1)
    moves[3].wait()


def restrict_body(v, pair, other, lower, upper, picks, basis, block, coef):
    edge = margins(lower[...], upper[...], pair[...], other[...], picks[...])
    whole = jnp.concatenate([v[...], edge], axis=1)
    block[...] = whole
    part = dot_nt(basis[...], tall(whole)).astype(BF16)
    for m in range(coef.shape[0]):
        coef[m] = part


def mixed_body(v, lower, upper, pair, other, picks, basis, edge, message):
    value = v[...]
    rows = jnp.concatenate([lower[...], upper[...]], axis=0)
    every = dot_nn(rows, picks[:, :LANES])
    lane = lanes((CASES, LANES))
    near = jnp.where(lane < HALF, every[:CASES], every[CASES:]).astype(BF16)
    edge[...] = near
    known = jnp.concatenate([value, near], axis=1)
    own = dot_nt(basis[:, : known.shape[1]], tall(known))
    width = 3 * LANES
    unfold = lambda ref: jnp.concatenate([ref[:, :width], ref[:, width:]], axis=0)
    first, second = unfold(pair), unfold(other)
    digits = (first[:1, LANES:] + second[:1, LANES:]).astype(F32)
    spot = (digits[:, :LANES] * DIGIT + digits[:, LANES:]).astype(jnp.int32)
    choice = lax.broadcasted_iota(jnp.int32, (value.shape[1], LANES), 0) == spot
    chosen = dot_nn(value, jnp.where(choice, 1.0, 0.0).astype(BF16))
    spread = tall(chosen.astype(BF16))
    to_first = dot_nt(first[:, :LANES], spread)
    to_second = dot_nt(second[:, :LANES], spread)
    head = own.astype(BF16).astype(F32)
    place = lanes(own.shape) // CASES
    out = jnp.concatenate([chosen, pltpu.roll(chosen, HALF, 1)], axis=0)
    out = jnp.where(place == 3, to_second, out)
    out = jnp.where(place == 2, to_first, out)
    out = jnp.where(place == 1, own - head, out)
    out = jnp.where(place == 0, head, out).astype(BF16)
    for m in range(message.shape[0]):
        message[m] = out


def shares_of(every, inverse, share):
    per = LANES // CASES
    lane = lanes(every.shape) // CASES
    tiles = inverse.shape[0] // per
    sums = [None] * tiles
    for q in range(per):
        here = jnp.where(lane == q, every, jnp.zeros_like(every))
        for t in range(tiles):
            term = dot_nn(inverse[per * t + q], here)
            sums[t] = term if sums[t] is None else sums[t] + term
    for t in range(tiles):
        share[:, t, :] = sums[t]


def coarse_body(coef, inverse, share):
    shares_of(coef[...].reshape(-1, LANES), inverse, share)


def coarse_mixed_body(message, inverse, share):
    peers, kdef, _ = message.shape
    source = lax.broadcasted_iota(jnp.int32, (LANES, 3 * LANES), 0)
    target = lanes((LANES, 3 * LANES))
    group = source // CASES
    part = jnp.where(group < 2, 0, group - 1)
    hit = (part == target // LANES) & (source % CASES == target % CASES)
    parts = dot_nn(message[...].reshape(peers * kdef, LANES), jnp.where(hit, 1.0, 0.0).astype(BF16))
    every = []
    for m in range(peers):
        pair = m ^ 1
        other = (m + 1) % peers if m % 2 else (m - 1) % peers
        at = lambda k, j: parts[k * kdef : (k + 1) * kdef, j * LANES : (j + 1) * LANES]
        every.append(at(m, 0) + at(pair, 1) + at(other, 2))
    shares_of(jnp.concatenate(every, axis=0).astype(BF16), inverse, share)


def prolong_of(arrived, kdef):
    total = jnp.sum(arrived, axis=0)
    tiles = total.shape[0]
    row = lax.broadcasted_iota(jnp.int32, (CASES, LANES), 0)
    lane = lanes((CASES, LANES))
    out = None
    for t in range(tiles):
        spread = jnp.where(lane % CASES == row, total[t : t + 1], 0.0).astype(BF16)
        target = lax.broadcasted_iota(jnp.int32, (LANES, kdef), 0) // CASES + t * (LANES // CASES)
        onto = (target == lanes((LANES, kdef))).astype(BF16)
        term = dot_nn(spread, onto)
        out = term if out is None else out + term
    return out.astype(BF16)


def correct_body(arrived, block, inverse, basis, for_pair, for_other, total, rounded, pair, other):
    value = dot_nt(block[...], inverse[...])
    prolong = prolong_of(arrived[...], basis.shape[0])
    value = value + dot_nn(prolong, basis[:, : total.shape[1]])
    total[...] = value
    short = value.astype(BF16)
    rounded[...] = short
    for out, more in ((pair, for_pair), (other, for_other)):
        out[:CASES] = short
        out[CASES:] = more[...]


def correct_mixed_body(arrived, v, edge, message, inverse, basis, before, total, rounded):
    me = lax.axis_index("member")
    peers = message.shape[0]
    even = even_member()
    pair = jnp.where(even, me + 1, me - 1)
    other = lax.rem(jnp.where(even, me + peers - 1, me + 1), peers)
    from_pair = message[pair, :CASES].astype(F32)
    from_other = message[other, CASES:].astype(F32)
    high = jnp.where(even, from_pair, from_other)
    low = jnp.where(even, from_other, from_pair)
    far = jnp.where(lanes(high.shape) < HALF, pltpu.roll(low, HALF, 1), high).astype(BF16)
    block = jnp.concatenate([v[...], edge[...], far], axis=1)
    value = dot_nt(block, inverse[...])
    prolong = prolong_of(arrived[...], basis.shape[0])
    value = before[...] + (value + dot_nn(prolong, basis[:, : total.shape[1]]))
    total[...] = value
    rounded[...] = value.astype(BF16)


def residual_body(last, v, pair, other, lower, upper, picks, stiff, load, *rest):
    edge = margins(lower[...], upper[...], pair[:CASES], other[:CASES], picks[...])
    whole = jnp.concatenate([v[...], edge], axis=1)
    value = load[...] - dot_nt(whole, stiff[...])
    if last:
        total, out, passed = rest
        passed[...] = total[...]
        out[...] = value
    else:
        out, from_pair, from_other = rest
        out[...] = value.astype(BF16)
        from_pair[...] = pair[CASES:]
        from_other[...] = other[CASES:]


def local(load, stiffness, block_inverse, deflation, margin_rows, coarse_inverse):
    own_load = load[0]
    stiff_rows = stiffness[0]
    inverse_rows = block_inverse[0]
    cases, owned = own_load.shape
    kdef, nb = deflation.shape[1:]
    groups = lax.axis_size("group")
    members = lax.axis_size("member")
    tiles = coarse_inverse.shape[0] * cases // LANES

    def group_around(values):
        lower = from_behind(values, "group", 1)
        upper = from_behind(values, "group", -1)
        return lower, upper

    def member_around(for_pair, for_other):
        pair = exchanged(for_pair, "member", 0)
        other = exchanged(for_other, "member", 1)
        return pair, other

    field, picks, basis, for_pair, for_other, inverse_coarse = call(
        begin_body,
        [((cases, owned), BF16), ((owned, nb - owned), BF16), ((kdef, nb), BF16)]
        + [((kdef // 2, 6 * LANES), BF16)] * 2
        + [(coarse_inverse.shape, BF16)],
        *(pltpu.with_memory_space_constraint(a, pltpu.HBM) for a in (own_load, margin_rows, deflation[0], coarse_inverse)),
        space=pltpu.HBM,
        scratch=(VMEM((cases, owned), F32), VMEM(margin_rows.shape, jnp.int32), pltpu.SemaphoreType.DMA((4,))),
    )
    near = member_around(field, field)
    far = group_around(field)
    block, coef = call(
        restrict_body,
        [((cases, nb), BF16), ((members, kdef, LANES), BF16)],
        field, *near, *far, picks, basis,
    )
    gathered = lax.all_to_all(coef, "member", 0, 0, tiled=True)
    share_shape = [((groups, tiles, LANES), F32)]
    (share,) = call(coarse_body, share_shape, gathered, inverse_coarse)
    arrived = lax.all_to_all(share, "group", 0, 0, tiled=True)
    total, rounded, for_pair, for_other = call(
        correct_body,
        [((cases, owned), F32), ((cases, owned), BF16)] + [((cases + kdef // 2, owned), BF16)] * 2,
        arrived, block, inverse_rows, basis, for_pair, for_other,
    )
    near = member_around(for_pair, for_other)
    field, from_pair, from_other = call(
        lambda *refs: residual_body(False, *refs),
        [((cases, owned), BF16)] + [((kdef // 2, owned), BF16)] * 2,
        rounded, *near, *group_around(rounded), picks, stiff_rows, own_load,
    )

    edge, message = call(
        mixed_body,
        [((cases, LANES), BF16), ((members, kdef, LANES), BF16)],
        field, *group_around(field), from_pair, from_other, picks, basis,
    )
    message = lax.all_to_all(message, "member", 0, 0, tiled=True)
    (share,) = call(coarse_mixed_body, share_shape, message, inverse_coarse)
    arrived = lax.all_to_all(share, "group", 0, 0, tiled=True)
    total, rounded = call(
        correct_mixed_body,
        [((cases, owned), F32), ((cases, owned), BF16)],
        arrived, field, edge, message, inverse_rows, basis, total,
    )
    residual, solution_out = call(
        lambda *refs: residual_body(True, *refs),
        [((cases, owned), F32)] * 2,
        rounded, *member_around(rounded, rounded), *group_around(rounded), picks, stiff_rows, own_load, total,
    )
    return (solution_out[None], residual[None])


def solution(mesh):
    placed = (
        P(("group", "member"), None, None),
        P(("group", "member"), None, None),
        P(("group", "member"), None, None),
        P(("group", "member"), None, None),
        P(("group", "member"), None, None),
        P("member", None, "group"),
    )
    return jax.shard_map(
        local,
        mesh=mesh,
        in_specs=placed,
        out_specs=(P(("group", "member"), None, None), P(("group", "member"), None, None)),
        check_vma=False,
    )
```

```python
import jax
import jax.numpy as jnp
from jax import lax
from jax.experimental import pallas as pl
from jax.experimental.pallas import tpu as pltpu
from jax.sharding import PartitionSpec as P


LANES = 128
HALF = 64
CASES = 16
DIGIT = 32
F32 = jnp.float32
BF16 = jnp.bfloat16
VMEM = pltpu.VMEM


def exchanged(shard, axis, first):
    peers = lax.axis_size(axis)
    pairs = [((first + i) % peers, (first + (i ^ 1)) % peers) for i in range(peers)]
    return lax.ppermute(shard, axis, pairs)


def call(body, outs, *args, space=VMEM, scratch=()):
    return pl.pallas_call(
        body,
        out_shape=[jax.ShapeDtypeStruct(shape, dtype) for shape, dtype in outs],
        in_specs=[pl.BlockSpec(memory_space=space)] * len(args),
        out_specs=[pl.BlockSpec(memory_space=VMEM)] * len(outs),
        scratch_shapes=list(scratch),
        compiler_params=pltpu.CompilerParams(vmem_limit_bytes=16 * 2**20),
    )(*args)


def dot_nt(left, right):
    return lax.dot_general(left, right, (((1,), (1,)), ((), ())), preferred_element_type=F32)


def dot_nn(left, right):
    return jnp.dot(left, right, preferred_element_type=F32)


def even(axis):
    return lax.rem(lax.axis_index(axis), 2) == 0


def tall(rows):
    return jnp.concatenate([rows] * (LANES // rows.shape[0]), axis=0)


def lanes(shape):
    return lax.broadcasted_iota(jnp.int32, shape, 1)


def margins(near, next_, pair, other, picks):
    every = dot_nn(jnp.concatenate([near, next_, pair, other], axis=0), picks)
    source = lanes((CASES, picks.shape[1])) // HALF
    by_group = jnp.where(even("group"), 1 - source, source)
    by_member = jnp.where(even("member"), 5 - source, source)
    owner = jnp.where(source < 2, by_group, by_member)
    kept = every[:CASES]
    for d in range(1, 4):
        kept = jnp.where(owner == d, every[d * CASES : (d + 1) * CASES], kept)
    return kept.astype(BF16)


def begin_body(far_load, far_rows, far_basis, far_inverse, field, picks, basis, for_pair, for_other, inverse,
               load, rows, sems):
    moves = [
        pltpu.make_async_copy(source, target, sems.at[i])
        for i, (source, target) in enumerate(
            ((far_load, load), (far_rows, rows), (far_basis, basis), (far_inverse, inverse))
        )
    ]
    for move in moves:
        move.start()
    moves[1].wait()
    lists = rows[0]
    nb = basis.shape[1]
    flat = jnp.concatenate([lists[d : d + 1] for d in range(4)], axis=1)
    spots = lax.broadcasted_iota(jnp.int32, picks.shape, 0)
    picks[...] = jnp.where(spots == flat, 1.0, 0.0).astype(BF16)
    moves[0].wait()
    field[...] = load[...].astype(BF16)
    moves[2].wait()
    upward = even("member")
    edge = basis[:, nb - LANES :].astype(F32)
    edge = jnp.where(upward, edge, pltpu.roll(edge, HALF, 1))
    turn = jnp.where(upward, flat[:, LANES:], jnp.concatenate([lists[3:4], lists[2:3]], axis=1))
    high = jnp.broadcast_to((turn // DIGIT).astype(F32), edge.shape)
    low = jnp.broadcast_to((turn % DIGIT).astype(F32), edge.shape)
    parts = jnp.concatenate([edge, high, low], axis=1)
    side = lanes(parts.shape) % LANES >= HALF
    half = parts.shape[0] // 2
    for out, mine in ((for_pair, side), (for_other, jnp.logical_not(side))):
        kept = jnp.where(mine, parts, 0.0).astype(BF16)
        out[...] = jnp.concatenate([kept[:half], kept[half:]], axis=1)
    moves[3].wait()


def restrict_body(v, pair, other, near, next_, picks, basis, block, coef):
    edge = margins(near[...], next_[...], pair[...], other[...], picks[...])
    whole = jnp.concatenate([v[...], edge], axis=1)
    block[...] = whole
    part = dot_nt(basis[...], tall(whole)).astype(BF16)
    for m in range(coef.shape[0]):
        coef[m] = part


def mixed_body(v, near, next_, pair, other, picks, basis, edge, message):
    value = v[...]
    rows = jnp.concatenate([near[...], next_[...]], axis=0)
    every = dot_nn(rows, picks[:, :LANES])
    lane = lanes((CASES, LANES))
    swapped = jnp.where(lane < HALF, every[CASES:], every[:CASES])
    straight = jnp.where(lane < HALF, every[:CASES], every[CASES:])
    beside = jnp.where(even("group"), swapped, straight).astype(BF16)
    edge[...] = beside
    known = jnp.concatenate([value, beside], axis=1)
    own = dot_nt(basis[:, : known.shape[1]], tall(known))
    width = 3 * LANES
    unfold = lambda ref: jnp.concatenate([ref[:, :width], ref[:, width:]], axis=0)
    first, second = unfold(pair), unfold(other)
    digits = (first[:1, LANES:] + second[:1, LANES:]).astype(F32)
    spot = (digits[:, :LANES] * DIGIT + digits[:, LANES:]).astype(jnp.int32)
    choice = lax.broadcasted_iota(jnp.int32, (value.shape[1], LANES), 0) == spot
    chosen = dot_nn(value, jnp.where(choice, 1.0, 0.0).astype(BF16))
    spread = tall(chosen.astype(BF16))
    to_first = dot_nt(first[:, :LANES], spread)
    to_second = dot_nt(second[:, :LANES], spread)
    head = own.astype(BF16).astype(F32)
    place = lanes(own.shape) // CASES
    out = jnp.concatenate([chosen, pltpu.roll(chosen, HALF, 1)], axis=0)
    out = jnp.where(place == 3, to_second, out)
    out = jnp.where(place == 2, to_first, out)
    out = jnp.where(place == 1, own - head, out)
    out = jnp.where(place == 0, head, out).astype(BF16)
    for m in range(message.shape[0]):
        message[m] = out


def shares_of(every, inverse, share):
    per = LANES // CASES
    lane = lanes(every.shape) // CASES
    tiles = inverse.shape[0] // per
    sums = [None] * tiles
    for q in range(per):
        here = jnp.where(lane == q, every, jnp.zeros_like(every))
        for t in range(tiles):
            term = dot_nn(inverse[per * t + q], here)
            sums[t] = term if sums[t] is None else sums[t] + term
    for t in range(tiles):
        share[:, t, :] = sums[t]


def coarse_body(coef, inverse, share):
    shares_of(coef[...].reshape(-1, LANES), inverse, share)


def coarse_mixed_body(message, inverse, share):
    peers, kdef, _ = message.shape
    source = lax.broadcasted_iota(jnp.int32, (LANES, 3 * LANES), 0)
    target = lanes((LANES, 3 * LANES))
    group = source // CASES
    part = jnp.where(group < 2, 0, group - 1)
    hit = (part == target // LANES) & (source % CASES == target % CASES)
    parts = dot_nn(message[...].reshape(peers * kdef, LANES), jnp.where(hit, 1.0, 0.0).astype(BF16))
    every = []
    for m in range(peers):
        pair = m ^ 1
        other = (m + 1) % peers if m % 2 else (m - 1) % peers
        at = lambda k, j: parts[k * kdef : (k + 1) * kdef, j * LANES : (j + 1) * LANES]
        every.append(at(m, 0) + at(pair, 1) + at(other, 2))
    shares_of(jnp.concatenate(every, axis=0).astype(BF16), inverse, share)


def prolong_of(arrived, kdef):
    total = jnp.sum(arrived, axis=0)
    tiles = total.shape[0]
    row = lax.broadcasted_iota(jnp.int32, (CASES, LANES), 0)
    lane = lanes((CASES, LANES))
    out = None
    for t in range(tiles):
        spread = jnp.where(lane % CASES == row, total[t : t + 1], 0.0).astype(BF16)
        target = lax.broadcasted_iota(jnp.int32, (LANES, kdef), 0) // CASES + t * (LANES // CASES)
        onto = (target == lanes((LANES, kdef))).astype(BF16)
        term = dot_nn(spread, onto)
        out = term if out is None else out + term
    return out.astype(BF16)


def correct_body(arrived, block, inverse, basis, for_pair, for_other, total, rounded, pair, other):
    value = dot_nt(block[...], inverse[...])
    prolong = prolong_of(arrived[...], basis.shape[0])
    value = value + dot_nn(prolong, basis[:, : total.shape[1]])
    total[...] = value
    short = value.astype(BF16)
    rounded[...] = short
    for out, more in ((pair, for_pair), (other, for_other)):
        out[:CASES] = short
        out[CASES:] = more[...]


def correct_mixed_body(arrived, v, edge, message, inverse, basis, before, total, rounded):
    me = lax.axis_index("member")
    peers = message.shape[0]
    upward = even("member")
    pair = jnp.where(upward, me + 1, me - 1)
    other = lax.rem(jnp.where(upward, me + peers - 1, me + 1), peers)
    from_pair = message[pair, :CASES].astype(F32)
    from_other = message[other, CASES:].astype(F32)
    high = jnp.where(upward, from_pair, from_other)
    low = jnp.where(upward, from_other, from_pair)
    far = jnp.where(lanes(high.shape) < HALF, pltpu.roll(low, HALF, 1), high).astype(BF16)
    block = jnp.concatenate([v[...], edge[...], far], axis=1)
    value = dot_nt(block, inverse[...])
    prolong = prolong_of(arrived[...], basis.shape[0])
    value = before[...] + (value + dot_nn(prolong, basis[:, : total.shape[1]]))
    total[...] = value
    rounded[...] = value.astype(BF16)


def residual_body(last, v, pair, other, near, next_, picks, stiff, load, *rest):
    edge = margins(near[...], next_[...], pair[:CASES], other[:CASES], picks[...])
    whole = jnp.concatenate([v[...], edge], axis=1)
    value = load[...] - dot_nt(whole, stiff[...])
    if last:
        total, out, passed = rest
        passed[...] = total[...]
        out[...] = value
    else:
        out, from_pair, from_other = rest
        out[...] = value.astype(BF16)
        from_pair[...] = pair[CASES:]
        from_other[...] = other[CASES:]


def local(load, stiffness, block_inverse, deflation, margin_rows, coarse_inverse):
    own_load = load[0]
    stiff_rows = stiffness[0]
    inverse_rows = block_inverse[0]
    cases, owned = own_load.shape
    kdef, nb = deflation.shape[1:]
    groups = lax.axis_size("group")
    members = lax.axis_size("member")
    tiles = coarse_inverse.shape[0] * cases // LANES

    def group_around(values):
        near = exchanged(values, "group", 0)
        next_ = exchanged(values, "group", 1)
        return near, next_

    def member_around(for_pair, for_other):
        pair = exchanged(for_pair, "member", 0)
        other = exchanged(for_other, "member", 1)
        return pair, other

    field, picks, basis, for_pair, for_other, inverse_coarse = call(
        begin_body,
        [((cases, owned), BF16), ((owned, nb - owned), BF16), ((kdef, nb), BF16)]
        + [((kdef // 2, 6 * LANES), BF16)] * 2
        + [(coarse_inverse.shape, BF16)],
        *(pltpu.with_memory_space_constraint(a, pltpu.HBM) for a in (own_load, margin_rows, deflation[0], coarse_inverse)),
        space=pltpu.HBM,
        scratch=(VMEM((cases, owned), F32), VMEM(margin_rows.shape, jnp.int32), pltpu.SemaphoreType.DMA((4,))),
    )
    near = member_around(field, field)
    far = group_around(field)
    block, coef = call(
        restrict_body,
        [((cases, nb), BF16), ((members, kdef, LANES), BF16)],
        field, *near, *far, picks, basis,
    )
    gathered = lax.all_to_all(coef, "member", 0, 0, tiled=True)
    share_shape = [((groups, tiles, LANES), F32)]
    (share,) = call(coarse_body, share_shape, gathered, inverse_coarse)
    arrived = lax.all_to_all(share, "group", 0, 0, tiled=True)
    total, rounded, for_pair, for_other = call(
        correct_body,
        [((cases, owned), F32), ((cases, owned), BF16)] + [((cases + kdef // 2, owned), BF16)] * 2,
        arrived, block, inverse_rows, basis, for_pair, for_other,
    )
    near = member_around(for_pair, for_other)
    field, from_pair, from_other = call(
        lambda *refs: residual_body(False, *refs),
        [((cases, owned), BF16)] + [((kdef // 2, owned), BF16)] * 2,
        rounded, *near, *group_around(rounded), picks, stiff_rows, own_load,
    )

    edge, message = call(
        mixed_body,
        [((cases, LANES), BF16), ((members, kdef, LANES), BF16)],
        field, *group_around(field), from_pair, from_other, picks, basis,
    )
    message = lax.all_to_all(message, "member", 0, 0, tiled=True)
    (share,) = call(coarse_mixed_body, share_shape, message, inverse_coarse)
    arrived = lax.all_to_all(share, "group", 0, 0, tiled=True)
    total, rounded = call(
        correct_mixed_body,
        [((cases, owned), F32), ((cases, owned), BF16)],
        arrived, field, edge, message, inverse_rows, basis, total,
    )
    residual, solution_out = call(
        lambda *refs: residual_body(True, *refs),
        [((cases, owned), F32)] * 2,
        rounded, *member_around(rounded, rounded), *group_around(rounded), picks, stiff_rows, own_load, total,
    )
    return (solution_out[None], residual[None])


def solution(mesh):
    placed = (
        P(("group", "member"), None, None),
        P(("group", "member"), None, None),
        P(("group", "member"), None, None),
        P(("group", "member"), None, None),
        P(("group", "member"), None, None),
        P("member", None, "group"),
    )
    return jax.shard_map(
        local,
        mesh=mesh,
        in_specs=placed,
        out_specs=(P(("group", "member"), None, None), P(("group", "member"), None, None)),
        check_vma=False,
    )
```

```python
import jax
import jax.numpy as jnp
from jax import lax
from jax.experimental import pallas as pl
from jax.experimental.pallas import tpu as pltpu
from jax.sharding import PartitionSpec as P


LANES = 128
HALF = 64
CASES = 16
DIGIT = 32
F32 = jnp.float32
BF16 = jnp.bfloat16
VMEM = pltpu.VMEM


def exchanged(shard, axis, first):
    peers = lax.axis_size(axis)
    pairs = [((first + i) % peers, (first + (i ^ 1)) % peers) for i in range(peers)]
    return lax.ppermute(shard, axis, pairs)


def call(body, outs, *args, space=VMEM, scratch=()):
    return pl.pallas_call(
        body,
        out_shape=[jax.ShapeDtypeStruct(shape, dtype) for shape, dtype in outs],
        in_specs=[pl.BlockSpec(memory_space=space)] * len(args),
        out_specs=[pl.BlockSpec(memory_space=VMEM)] * len(outs),
        scratch_shapes=list(scratch),
        compiler_params=pltpu.CompilerParams(vmem_limit_bytes=16 * 2**20),
    )(*args)


def dot_nt(left, right):
    return lax.dot_general(left, right, (((1,), (1,)), ((), ())), preferred_element_type=F32)


def dot_nn(left, right):
    return jnp.dot(left, right, preferred_element_type=F32)


def even(axis):
    return lax.rem(lax.axis_index(axis), 2) == 0


def tall(rows):
    return jnp.concatenate([rows] * (LANES // rows.shape[0]), axis=0)


def lanes(shape):
    return lax.broadcasted_iota(jnp.int32, shape, 1)


def margins(near, next_, pair, other, picks):
    every = dot_nn(jnp.concatenate([near, next_, pair, other], axis=0), picks)
    source = lanes((CASES, picks.shape[1])) // HALF
    by_group = jnp.where(even("group"), 1 - source, source)
    by_member = jnp.where(even("member"), 5 - source, source)
    owner = jnp.where(source < 2, by_group, by_member)
    kept = every[:CASES]
    for d in range(1, 4):
        kept = jnp.where(owner == d, every[d * CASES : (d + 1) * CASES], kept)
    return kept.astype(BF16)


def two_margins(near, next_, picks, axis):
    every = dot_nn(jnp.concatenate([near, next_], axis=0), picks)
    lane = lanes((CASES, LANES))
    swapped = jnp.where(lane < HALF, every[CASES:], every[:CASES])
    straight = jnp.where(lane < HALF, every[:CASES], every[CASES:])
    return jnp.where(even(axis), swapped, straight).astype(BF16)


def one_hot(digits, rows):
    spot = (digits[:, :LANES] * DIGIT + digits[:, LANES:]).astype(jnp.int32)
    choice = lax.broadcasted_iota(jnp.int32, (rows, LANES), 0) == spot
    return jnp.where(choice, 1.0, 0.0).astype(BF16)


def partners(axis, peers):
    me = lax.axis_index(axis)
    upward = even(axis)
    return jnp.where(upward, me + 1, me - 1), lax.rem(jnp.where(upward, me + peers - 1, me + 1), peers)


def begin_body(far_load, far_rows, far_basis, far_inverse, field, picks, basis, for_pair, for_other, for_group, inverse,
               load, rows, sems):
    moves = [
        pltpu.make_async_copy(source, target, sems.at[i])
        for i, (source, target) in enumerate(
            ((far_load, load), (far_rows, rows), (far_basis, basis), (far_inverse, inverse))
        )
    ]
    for move in moves:
        move.start()
    moves[1].wait()
    lists = rows[0]
    nb = basis.shape[1]
    flat = jnp.concatenate([lists[d : d + 1] for d in range(4)], axis=1)
    spots = lax.broadcasted_iota(jnp.int32, picks.shape, 0)
    picks[...] = jnp.where(spots == flat, 1.0, 0.0).astype(BF16)
    moves[0].wait()
    field[...] = load[...].astype(BF16)
    moves[2].wait()
    upward = even("member")
    edge = basis[:, nb - LANES :].astype(F32)
    edge = jnp.where(upward, edge, pltpu.roll(edge, HALF, 1))
    turn = jnp.where(upward, flat[:, LANES:], jnp.concatenate([lists[3:4], lists[2:3]], axis=1))
    around = jnp.where(even("group"), flat[:, :LANES], jnp.concatenate([lists[1:2], lists[0:1]], axis=1))
    tens = (around // DIGIT).astype(F32)
    ones = (around % DIGIT).astype(F32)
    pad = jnp.zeros((1, for_group.shape[1] - 2 * LANES), F32)
    digits = jnp.concatenate([tens, ones, pad], axis=1)
    for_group[...] = jnp.broadcast_to(digits, for_group.shape).astype(BF16)
    high = jnp.broadcast_to((turn // DIGIT).astype(F32), edge.shape)
    low = jnp.broadcast_to((turn % DIGIT).astype(F32), edge.shape)
    parts = jnp.concatenate([edge, high, low], axis=1)
    side = lanes(parts.shape) % LANES >= HALF
    half = parts.shape[0] // 2
    for out, mine in ((for_pair, side), (for_other, jnp.logical_not(side))):
        kept = jnp.where(mine, parts, 0.0).astype(BF16)
        out[...] = jnp.concatenate([kept[:half], kept[half:]], axis=1)
    moves[3].wait()


def restrict_body(v, pair, other, near, next_, picks, basis, block, coef):
    edge = margins(near[...], next_[...], pair[...], other[...], picks[...])
    whole = jnp.concatenate([v[...], edge], axis=1)
    block[...] = whole
    part = dot_nt(basis[...], tall(whole)).astype(BF16)
    for m in range(coef.shape[0]):
        coef[m] = part


def mixed_body(v, near, next_, pair, other, picks, basis, edge, message):
    value = v[:CASES]
    beside = two_margins(near[:CASES], next_[:CASES], picks[:, :LANES], "group")
    edge[...] = beside
    known = jnp.concatenate([value, beside], axis=1)
    own = dot_nt(basis[:, : known.shape[1]], tall(known))
    width = 3 * LANES
    unfold = lambda ref: jnp.concatenate([ref[:, :width], ref[:, width:]], axis=0)
    first, second = unfold(pair), unfold(other)
    digits = (first[:1, LANES:] + second[:1, LANES:]).astype(F32)
    chosen = dot_nn(value, one_hot(digits, value.shape[1]))
    spread = tall(chosen.astype(BF16))
    to_first = dot_nt(first[:, :LANES], spread)
    to_second = dot_nt(second[:, :LANES], spread)
    head = own.astype(BF16).astype(F32)
    place = lanes(own.shape) // CASES
    out = jnp.concatenate([chosen, pltpu.roll(chosen, HALF, 1)], axis=0)
    out = jnp.where(place == 3, to_second, out)
    out = jnp.where(place == 2, to_first, out)
    out = jnp.where(place == 1, own - head, out)
    out = jnp.where(place == 0, head, out).astype(BF16)
    for m in range(message.shape[0]):
        message[m] = out


def shares_of(every, inverse, share):
    per = LANES // CASES
    lane = lanes(every.shape) // CASES
    tiles = inverse.shape[0] // per
    sums = [None] * tiles
    for q in range(per):
        here = jnp.where(lane == q, every, jnp.zeros_like(every))
        for t in range(tiles):
            term = dot_nn(inverse[per * t + q], here)
            sums[t] = term if sums[t] is None else sums[t] + term
    for t in range(tiles):
        share[:, t, :] = sums[t]


def coarse_body(coef, inverse, share):
    shares_of(coef[...].reshape(-1, LANES), inverse, share)


def coarse_mixed_body(message, inverse, v, edge, inverse_rows, before, choice, out, total, share):
    peers, kdef, _ = message.shape
    source = lax.broadcasted_iota(jnp.int32, (LANES, 3 * LANES), 0)
    target = lanes((LANES, 3 * LANES))
    group = source // CASES
    part = jnp.where(group < 2, 0, group - 1)
    hit = (part == target // LANES) & (source % CASES == target % CASES)
    parts = dot_nn(message[...].reshape(peers * kdef, LANES), jnp.where(hit, 1.0, 0.0).astype(BF16))
    every = []
    for m in range(peers):
        pair = m ^ 1
        other = (m + 1) % peers if m % 2 else (m - 1) % peers
        at = lambda k, j: parts[k * kdef : (k + 1) * kdef, j * LANES : (j + 1) * LANES]
        every.append(at(m, 0) + at(pair, 1) + at(other, 2))
    shares_of(jnp.concatenate(every, axis=0).astype(BF16), inverse, share)
    pair, other = partners("member", peers)
    from_pair = message[pair, :CASES].astype(F32)
    from_other = message[other, CASES:].astype(F32)
    upward = even("member")
    high = jnp.where(upward, from_pair, from_other)
    low = jnp.where(upward, from_other, from_pair)
    left = lanes(high.shape) < HALF
    far = jnp.where(left, pltpu.roll(low, HALF, 1), high).astype(BF16)
    block = jnp.concatenate([v[:CASES], edge[...], far], axis=1)
    value = before[...] + dot_nt(block, inverse_rows[...])
    total[...] = value
    short = share[...].astype(BF16)
    groups = short.shape[0]
    out[:, 0] = short
    out[1:, 1] = short[:-1]
    out[:1, 1] = short[-1:]
    out[:-1, 2] = short[1:]
    out[-1:, 2] = short[:1]
    out[:, 3:] = jnp.zeros((groups, 2) + short.shape[1:], BF16)
    chosen = dot_nn(value.astype(BF16), choice[...])
    top, low = chosen[: CASES // 2], pltpu.roll(chosen, HALF, 1)[CASES // 2 :]
    side = lanes(top.shape) < HALF
    near, next_ = partners("group", groups)
    rows = short.shape[1]
    for target, kept in ((near, jnp.where(side, low, top)), (next_, jnp.where(side, top, low))):
        kept = kept.astype(BF16)
        out[target, 3] = kept[:rows]
        out[target, 4] = kept[rows:]


def prolong_of(arrived, kdef):
    total = jnp.sum(arrived, axis=0)
    tiles = total.shape[0]
    row = lax.broadcasted_iota(jnp.int32, (CASES, LANES), 0)
    lane = lanes((CASES, LANES))
    out = None
    for t in range(tiles):
        spread = jnp.where(lane % CASES == row, total[t : t + 1], 0.0).astype(BF16)
        target = lax.broadcasted_iota(jnp.int32, (LANES, kdef), 0) // CASES + t * (LANES // CASES)
        onto = (target == lanes((LANES, kdef))).astype(BF16)
        term = dot_nn(spread, onto)
        out = term if out is None else out + term
    return out.astype(BF16)


def correct_body(arrived, block, inverse, basis, for_pair, for_other, for_group, total, rounded, pair, other, group):
    value = dot_nt(block[...], inverse[...])
    prolong = prolong_of(arrived[...], basis.shape[0])
    value = value + dot_nn(prolong, basis[:, : total.shape[1]])
    total[...] = value
    short = value.astype(BF16)
    rounded[...] = short
    for out, more in ((pair, for_pair), (other, for_other), (group, for_group)):
        out[:CASES] = short
        out[CASES:] = more[...]


def correct_mixed_body(arrived, before, near, next_, basis, total, rounded, edge):
    kdef = basis.shape[0]
    upward = even("group")
    first, second = partners("group", arrived.shape[0])
    take = lambda k: jnp.concatenate([arrived[k, 3], arrived[k, 4]], axis=0).astype(F32)
    widen = lambda part: jnp.concatenate([part, pltpu.roll(part, HALF, 1)], axis=0)
    left = lanes((CASES, LANES)) < HALF
    known = jnp.where(left, widen(take(second)), widen(take(first)))
    known = jnp.where(upward, known, pltpu.roll(known, HALF, 1))
    unfold = lambda ref: jnp.concatenate([ref[CASES:, :LANES], ref[CASES:, LANES : 2 * LANES]], axis=0)
    vectors = jnp.where(lanes((kdef, LANES)) < HALF, unfold(next_).astype(F32), unfold(near).astype(F32))
    vectors = jnp.where(upward, vectors, pltpu.roll(vectors, HALF, 1)).astype(BF16)
    prolong = [prolong_of(arrived[:, k].astype(F32), kdef) for k in range(3)]
    added = jnp.where(left, dot_nn(prolong[1], vectors), dot_nn(prolong[2], vectors))
    edge[...] = (known + added).astype(BF16)
    value = before[...] + dot_nn(prolong[0], basis[:, : total.shape[1]])
    total[...] = value
    rounded[...] = value.astype(BF16)


def residual_body(v, pair, other, near, next_, picks, basis, stiff, load, group, from_pair, from_other, choice):
    edge = margins(near[:CASES], next_[:CASES], pair[:CASES], other[:CASES], picks[...])
    whole = jnp.concatenate([v[...], edge], axis=1)
    value = load[...] - dot_nt(whole, stiff[...])
    from_pair[...] = pair[CASES:]
    from_other[...] = other[CASES:]
    owned = value.shape[1]
    left = lanes((1, 2 * LANES)) % LANES < HALF
    told = lambda ref: ref[CASES : CASES + 1, : 2 * LANES].astype(F32)
    chosen = one_hot(jnp.where(left, told(next_), told(near)), owned)
    choice[...] = chosen
    vectors = dot_nn(basis[:, :owned], chosen).astype(BF16)
    pad = jnp.zeros((CASES, owned - 2 * LANES), BF16)
    group[:CASES] = value.astype(BF16)
    group[CASES:] = jnp.concatenate([vectors[:CASES], vectors[CASES:], pad], axis=1)


def finish_body(v, pair, other, edge, picks, stiff, load, total, out, passed):
    far = two_margins(pair[...], other[...], picks[:, LANES:], "member")
    whole = jnp.concatenate([v[...], edge[...], far], axis=1)
    passed[...] = total[...]
    out[...] = load[...] - dot_nt(whole, stiff[...])


def local(load, stiffness, block_inverse, deflation, margin_rows, coarse_inverse):
    own_load = load[0]
    stiff_rows = stiffness[0]
    inverse_rows = block_inverse[0]
    cases, owned = own_load.shape
    kdef, nb = deflation.shape[1:]
    groups = lax.axis_size("group")
    members = lax.axis_size("member")
    tiles = coarse_inverse.shape[0] * cases // LANES

    def group_around(values):
        near = exchanged(values, "group", 0)
        next_ = exchanged(values, "group", 1)
        return near, next_

    def member_around(for_pair, for_other):
        pair = exchanged(for_pair, "member", 0)
        other = exchanged(for_other, "member", 1)
        return pair, other

    field, picks, basis, for_pair, for_other, for_group, inverse_coarse = call(
        begin_body,
        [((cases, owned), BF16), ((owned, nb - owned), BF16), ((kdef, nb), BF16)]
        + [((kdef // 2, owned), BF16)] * 3
        + [(coarse_inverse.shape, BF16)],
        *(pltpu.with_memory_space_constraint(a, pltpu.HBM) for a in (own_load, margin_rows, deflation[0], coarse_inverse)),
        space=pltpu.HBM,
        scratch=(VMEM((cases, owned), F32), VMEM(margin_rows.shape, jnp.int32), pltpu.SemaphoreType.DMA((4,))),
    )
    near = member_around(field, field)
    far = group_around(field)
    block, coef = call(
        restrict_body,
        [((cases, nb), BF16), ((members, kdef, LANES), BF16)],
        field, *near, *far, picks, basis,
    )
    gathered = lax.all_to_all(coef, "member", 0, 0, tiled=True)
    share_shape = [((groups, tiles, LANES), F32)]
    (share,) = call(coarse_body, share_shape, gathered, inverse_coarse)
    arrived = lax.all_to_all(share, "group", 0, 0, tiled=True)
    total, rounded, for_pair, for_other, for_group = call(
        correct_body,
        [((cases, owned), F32), ((cases, owned), BF16)] + [((cases + kdef // 2, owned), BF16)] * 3,
        arrived, block, inverse_rows, basis, for_pair, for_other, for_group,
    )
    near = member_around(for_pair, for_other)
    field, from_pair, from_other, choice = call(
        residual_body,
        [((cases + kdef // 2, owned), BF16)] + [((kdef // 2, owned), BF16)] * 2 + [((owned, LANES), BF16)],
        rounded, *near, *group_around(for_group), picks, basis, stiff_rows, own_load,
    )

    far = group_around(field)
    edge, message = call(
        mixed_body,
        [((cases, LANES), BF16), ((members, kdef, LANES), BF16)],
        field, *far, from_pair, from_other, picks, basis,
    )
    message = lax.all_to_all(message, "member", 0, 0, tiled=True)
    share, total = call(
        coarse_mixed_body,
        [((groups, 5, tiles, LANES), BF16), ((cases, owned), F32)],
        message, inverse_coarse, field, edge, inverse_rows, total, choice,
        scratch=(VMEM((groups, tiles, LANES), F32),),
    )
    arrived = lax.all_to_all(share, "group", 0, 0, tiled=True)
    total, rounded, edge = call(
        correct_mixed_body,
        [((cases, owned), F32), ((cases, owned), BF16), ((cases, LANES), BF16)],
        arrived, total, *far, basis,
    )
    residual, solution_out = call(
        finish_body,
        [((cases, owned), F32)] * 2,
        rounded, *member_around(rounded, rounded), edge, picks, stiff_rows, own_load, total,
    )
    return (solution_out[None], residual[None])


def solution(mesh):
    placed = (
        P(("group", "member"), None, None),
        P(("group", "member"), None, None),
        P(("group", "member"), None, None),
        P(("group", "member"), None, None),
        P(("group", "member"), None, None),
        P("member", None, "group"),
    )
    return jax.shard_map(
        local,
        mesh=mesh,
        in_specs=placed,
        out_specs=(P(("group", "member"), None, None), P(("group", "member"), None, None)),
        check_vma=False,
    )
```

```python
import jax
import jax.numpy as jnp
from jax import lax
from jax.experimental import pallas as pl
from jax.experimental.pallas import tpu as pltpu
from jax.sharding import PartitionSpec as P


LANES = 128
HALF = 64
CASES = 16
DIGIT = 32
F32 = jnp.float32
BF16 = jnp.bfloat16
VMEM = pltpu.VMEM


def exchanged(shard, axis, first):
    peers = lax.axis_size(axis)
    pairs = [((first + i) % peers, (first + (i ^ 1)) % peers) for i in range(peers)]
    return lax.ppermute(shard, axis, pairs)


def call(body, outs, *args, space=VMEM, scratch=()):
    return pl.pallas_call(
        body,
        out_shape=[jax.ShapeDtypeStruct(shape, dtype) for shape, dtype in outs],
        in_specs=[pl.BlockSpec(memory_space=space)] * len(args),
        out_specs=[pl.BlockSpec(memory_space=VMEM)] * len(outs),
        scratch_shapes=list(scratch),
        compiler_params=pltpu.CompilerParams(vmem_limit_bytes=16 * 2**20),
    )(*args)


def dot_nt(left, right):
    return lax.dot_general(left, right, (((1,), (1,)), ((), ())), preferred_element_type=F32)


def dot_nn(left, right):
    return jnp.dot(left, right, preferred_element_type=F32)


def even(axis):
    return lax.rem(lax.axis_index(axis), 2) == 0


def tall(rows):
    return jnp.concatenate([rows] * (LANES // rows.shape[0]), axis=0)


def lanes(shape):
    return lax.broadcasted_iota(jnp.int32, shape, 1)


def margins(near, next_, pair, other, picks):
    every = dot_nn(jnp.concatenate([near, next_, pair, other], axis=0), picks)
    source = lanes((CASES, picks.shape[1])) // HALF
    by_group = jnp.where(even("group"), 1 - source, source)
    by_member = jnp.where(even("member"), 5 - source, source)
    owner = jnp.where(source < 2, by_group, by_member)
    kept = every[:CASES]
    for d in range(1, 4):
        kept = jnp.where(owner == d, every[d * CASES : (d + 1) * CASES], kept)
    return kept.astype(BF16)


def two_margins(near, next_, picks, axis):
    every = dot_nn(jnp.concatenate([near, next_], axis=0), picks)
    lane = lanes((CASES, LANES))
    swapped = jnp.where(lane < HALF, every[CASES:], every[:CASES])
    straight = jnp.where(lane < HALF, every[:CASES], every[CASES:])
    return jnp.where(even(axis), swapped, straight).astype(BF16)


def one_hot(digits, rows):
    spot = (digits[:, :LANES] * DIGIT + digits[:, LANES:]).astype(jnp.int32)
    choice = lax.broadcasted_iota(jnp.int32, (rows, LANES), 0) == spot
    return jnp.where(choice, 1.0, 0.0).astype(BF16)


def partners(axis, peers):
    me = lax.axis_index(axis)
    upward = even(axis)
    return jnp.where(upward, me + 1, me - 1), lax.rem(jnp.where(upward, me + peers - 1, me + 1), peers)


def begin_body(far_load, far_rows, far_basis, far_inverse, field, picks, basis, for_pair, for_other, for_group, inverse,
               load, rows, sems):
    moves = [
        pltpu.make_async_copy(source, target, sems.at[i])
        for i, (source, target) in enumerate(
            ((far_load, load), (far_rows, rows), (far_basis, basis), (far_inverse, inverse))
        )
    ]
    for move in moves:
        move.start()
    moves[1].wait()
    lists = rows[0]
    nb = basis.shape[1]
    flat = jnp.concatenate([lists[d : d + 1] for d in range(4)], axis=1)
    spots = lax.broadcasted_iota(jnp.int32, picks.shape, 0)
    picks[...] = jnp.where(spots == flat, 1.0, 0.0).astype(BF16)
    moves[0].wait()
    field[...] = load[...].astype(BF16)
    moves[2].wait()
    upward = even("member")
    edge = basis[:, nb - LANES :].astype(F32)
    edge = jnp.where(upward, edge, pltpu.roll(edge, HALF, 1))
    turn = jnp.where(upward, flat[:, LANES:], jnp.concatenate([lists[3:4], lists[2:3]], axis=1))
    around = jnp.where(even("group"), flat[:, :LANES], jnp.concatenate([lists[1:2], lists[0:1]], axis=1))
    tens = (around // DIGIT).astype(F32)
    ones = (around % DIGIT).astype(F32)
    pad = jnp.zeros((1, for_group.shape[1] - 2 * LANES), F32)
    digits = jnp.concatenate([tens, ones, pad], axis=1)
    for_group[...] = jnp.broadcast_to(digits, for_group.shape).astype(BF16)
    high = jnp.broadcast_to((turn // DIGIT).astype(F32), edge.shape)
    low = jnp.broadcast_to((turn % DIGIT).astype(F32), edge.shape)
    parts = jnp.concatenate([edge, high, low], axis=1)
    side = lanes(parts.shape) % LANES >= HALF
    half = parts.shape[0] // 2
    for out, mine in ((for_pair, side), (for_other, jnp.logical_not(side))):
        kept = jnp.where(mine, parts, 0.0).astype(BF16)
        out[...] = jnp.concatenate([kept[:half], kept[half:]], axis=1)
    moves[3].wait()


def restrict_body(v, pair, other, near, next_, picks, basis, block, coef):
    fields = [ref[...].astype(BF16) for ref in (near, next_, pair, other)]
    whole = jnp.concatenate([v[...], margins(*fields, picks[...])], axis=1)
    block[...] = whole
    part = dot_nt(basis[...], tall(whole)).astype(BF16)
    for m in range(coef.shape[0]):
        coef[m] = part


def mixed_body(v, near, next_, pair, other, picks, basis, edge, message):
    value = v[:CASES]
    beside = two_margins(near[:CASES], next_[:CASES], picks[:, :LANES], "group")
    edge[...] = beside
    known = jnp.concatenate([value, beside], axis=1)
    own = dot_nt(basis[:, : known.shape[1]], tall(known))
    width = 3 * LANES
    unfold = lambda ref: jnp.concatenate([ref[:, :width], ref[:, width:]], axis=0)
    first, second = unfold(pair), unfold(other)
    digits = (first[:1, LANES:] + second[:1, LANES:]).astype(F32)
    chosen = dot_nn(value, one_hot(digits, value.shape[1]))
    spread = tall(chosen.astype(BF16))
    to_first = dot_nt(first[:, :LANES], spread)
    to_second = dot_nt(second[:, :LANES], spread)
    head = own.astype(BF16).astype(F32)
    place = lanes(own.shape) // CASES
    out = jnp.concatenate([chosen, pltpu.roll(chosen, HALF, 1)], axis=0)
    out = jnp.where(place == 3, to_second, out)
    out = jnp.where(place == 2, to_first, out)
    out = jnp.where(place == 1, own - head, out)
    out = jnp.where(place == 0, head, out).astype(BF16)
    for m in range(message.shape[0]):
        message[m] = out


def shares_of(every, inverse, share):
    per = LANES // CASES
    lane = lanes(every.shape) // CASES
    tiles = inverse.shape[0] // per
    sums = [None] * tiles
    for q in range(per):
        here = jnp.where(lane == q, every, jnp.zeros_like(every))
        for t in range(tiles):
            term = dot_nn(inverse[per * t + q], here)
            sums[t] = term if sums[t] is None else sums[t] + term
    for t in range(tiles):
        share[:, t, :] = sums[t]


def coarse_body(coef, inverse, share):
    shares_of(coef[...].reshape(-1, LANES), inverse, share)


def coarse_mixed_body(message, inverse, v, edge, inverse_rows, before, choice, out, total, share):
    peers, kdef, _ = message.shape
    source = lax.broadcasted_iota(jnp.int32, (LANES, 3 * LANES), 0)
    target = lanes((LANES, 3 * LANES))
    group = source // CASES
    part = jnp.where(group < 2, 0, group - 1)
    hit = (part == target // LANES) & (source % CASES == target % CASES)
    parts = dot_nn(message[...].reshape(peers * kdef, LANES), jnp.where(hit, 1.0, 0.0).astype(BF16))
    every = []
    for m in range(peers):
        pair = m ^ 1
        other = (m + 1) % peers if m % 2 else (m - 1) % peers
        at = lambda k, j: parts[k * kdef : (k + 1) * kdef, j * LANES : (j + 1) * LANES]
        every.append(at(m, 0) + at(pair, 1) + at(other, 2))
    shares_of(jnp.concatenate(every, axis=0).astype(BF16), inverse, share)
    pair, other = partners("member", peers)
    from_pair = message[pair, :CASES].astype(F32)
    from_other = message[other, CASES:].astype(F32)
    upward = even("member")
    high = jnp.where(upward, from_pair, from_other)
    low = jnp.where(upward, from_other, from_pair)
    left = lanes(high.shape) < HALF
    far = jnp.where(left, pltpu.roll(low, HALF, 1), high).astype(BF16)
    block = jnp.concatenate([v[:CASES], edge[...], far], axis=1)
    value = before[...] + dot_nt(block, inverse_rows[...])
    total[...] = value
    short = share[...].astype(BF16)
    groups = short.shape[0]
    out[:, 0] = short
    out[1:, 1] = short[:-1]
    out[:1, 1] = short[-1:]
    out[:-1, 2] = short[1:]
    out[-1:, 2] = short[:1]
    out[:, 3:] = jnp.zeros((groups, 2) + short.shape[1:], BF16)
    chosen = dot_nn(value.astype(BF16), choice[...])
    top, low = chosen[: CASES // 2], pltpu.roll(chosen, HALF, 1)[CASES // 2 :]
    side = lanes(top.shape) < HALF
    near, next_ = partners("group", groups)
    rows = short.shape[1]
    for target, kept in ((near, jnp.where(side, low, top)), (next_, jnp.where(side, top, low))):
        kept = kept.astype(BF16)
        out[target, 3] = kept[:rows]
        out[target, 4] = kept[rows:]


def prolong_of(arrived, kdef):
    total = jnp.sum(arrived, axis=0)
    tiles = total.shape[0]
    row = lax.broadcasted_iota(jnp.int32, (CASES, LANES), 0)
    lane = lanes((CASES, LANES))
    out = None
    for t in range(tiles):
        spread = jnp.where(lane % CASES == row, total[t : t + 1], 0.0).astype(BF16)
        target = lax.broadcasted_iota(jnp.int32, (LANES, kdef), 0) // CASES + t * (LANES // CASES)
        onto = (target == lanes((LANES, kdef))).astype(BF16)
        term = dot_nn(spread, onto)
        out = term if out is None else out + term
    return out.astype(BF16)


def correct_body(arrived, block, inverse, basis, for_pair, for_other, for_group, total, rounded, pair, other, group):
    value = dot_nt(block[...], inverse[...])
    prolong = prolong_of(arrived[...], basis.shape[0])
    value = value + dot_nn(prolong, basis[:, : total.shape[1]])
    total[...] = value
    short = value.astype(BF16)
    rounded[...] = short
    for out, more in ((pair, for_pair), (other, for_other), (group, for_group)):
        out[:CASES] = short
        out[CASES:] = more[...]


def correct_mixed_body(arrived, before, near, next_, basis, total, rounded, edge):
    kdef = basis.shape[0]
    upward = even("group")
    first, second = partners("group", arrived.shape[0])
    take = lambda k: jnp.concatenate([arrived[k, 3], arrived[k, 4]], axis=0).astype(F32)
    widen = lambda part: jnp.concatenate([part, pltpu.roll(part, HALF, 1)], axis=0)
    left = lanes((CASES, LANES)) < HALF
    known = jnp.where(left, widen(take(second)), widen(take(first)))
    known = jnp.where(upward, known, pltpu.roll(known, HALF, 1))
    unfold = lambda ref: jnp.concatenate([ref[CASES:, :LANES], ref[CASES:, LANES : 2 * LANES]], axis=0)
    vectors = jnp.where(lanes((kdef, LANES)) < HALF, unfold(next_).astype(F32), unfold(near).astype(F32))
    vectors = jnp.where(upward, vectors, pltpu.roll(vectors, HALF, 1)).astype(BF16)
    prolong = [prolong_of(arrived[:, k].astype(F32), kdef) for k in range(3)]
    added = jnp.where(left, dot_nn(prolong[1], vectors), dot_nn(prolong[2], vectors))
    edge[...] = (known + added).astype(BF16)
    value = before[...] + dot_nn(prolong[0], basis[:, : total.shape[1]])
    total[...] = value
    rounded[...] = value.astype(BF16)


def residual_body(v, pair, other, near, next_, picks, basis, stiff, load, group, from_pair, from_other, choice):
    edge = margins(near[:CASES], next_[:CASES], pair[:CASES], other[:CASES], picks[...])
    whole = jnp.concatenate([v[...], edge], axis=1)
    value = load[...] - dot_nt(whole, stiff[...])
    from_pair[...] = pair[CASES:]
    from_other[...] = other[CASES:]
    owned = value.shape[1]
    left = lanes((1, 2 * LANES)) % LANES < HALF
    told = lambda ref: ref[CASES : CASES + 1, : 2 * LANES].astype(F32)
    chosen = one_hot(jnp.where(left, told(next_), told(near)), owned)
    choice[...] = chosen
    vectors = dot_nn(basis[:, :owned], chosen).astype(BF16)
    pad = jnp.zeros((CASES, owned - 2 * LANES), BF16)
    group[:CASES] = value.astype(BF16)
    group[CASES:] = jnp.concatenate([vectors[:CASES], vectors[CASES:], pad], axis=1)


def finish_body(v, pair, other, edge, picks, stiff, load, total, out, passed):
    far = two_margins(pair[...], other[...], picks[:, LANES:], "member")
    whole = jnp.concatenate([v[...], edge[...], far], axis=1)
    passed[...] = total[...]
    out[...] = load[...] - dot_nt(whole, stiff[...])


def local(load, stiffness, block_inverse, deflation, margin_rows, coarse_inverse):
    own_load = load[0]
    stiff_rows = stiffness[0]
    inverse_rows = block_inverse[0]
    cases, owned = own_load.shape
    kdef, nb = deflation.shape[1:]
    groups = lax.axis_size("group")
    members = lax.axis_size("member")
    tiles = coarse_inverse.shape[0] * cases // LANES

    def group_around(values):
        near = exchanged(values, "group", 0)
        next_ = exchanged(values, "group", 1)
        return near, next_

    def member_around(for_pair, for_other):
        pair = exchanged(for_pair, "member", 0)
        other = exchanged(for_other, "member", 1)
        return pair, other

    field, picks, basis, for_pair, for_other, for_group, inverse_coarse = call(
        begin_body,
        [((cases, owned), BF16), ((owned, nb - owned), BF16), ((kdef, nb), BF16)]
        + [((kdef // 2, owned), BF16)] * 3
        + [(coarse_inverse.shape, BF16)],
        *(pltpu.with_memory_space_constraint(a, pltpu.HBM) for a in (own_load, margin_rows, deflation[0], coarse_inverse)),
        space=pltpu.HBM,
        scratch=(VMEM((cases, owned), F32), VMEM(margin_rows.shape, jnp.int32), pltpu.SemaphoreType.DMA((4,))),
    )
    near = member_around(own_load, own_load)
    far = group_around(own_load)
    block, coef = call(
        restrict_body,
        [((cases, nb), BF16), ((members, kdef, LANES), BF16)],
        field, *near, *far, picks, basis,
    )
    gathered = lax.all_to_all(coef, "member", 0, 0, tiled=True)
    share_shape = [((groups, tiles, LANES), F32)]
    (share,) = call(coarse_body, share_shape, gathered, inverse_coarse)
    arrived = lax.all_to_all(share, "group", 0, 0, tiled=True)
    total, rounded, for_pair, for_other, for_group = call(
        correct_body,
        [((cases, owned), F32), ((cases, owned), BF16)] + [((cases + kdef // 2, owned), BF16)] * 3,
        arrived, block, inverse_rows, basis, for_pair, for_other, for_group,
    )
    near = member_around(for_pair, for_other)
    field, from_pair, from_other, choice = call(
        residual_body,
        [((cases + kdef // 2, owned), BF16)] + [((kdef // 2, owned), BF16)] * 2 + [((owned, LANES), BF16)],
        rounded, *near, *group_around(for_group), picks, basis, stiff_rows, own_load,
    )

    far = group_around(field)
    edge, message = call(
        mixed_body,
        [((cases, LANES), BF16), ((members, kdef, LANES), BF16)],
        field, *far, from_pair, from_other, picks, basis,
    )
    message = lax.all_to_all(message, "member", 0, 0, tiled=True)
    share, total = call(
        coarse_mixed_body,
        [((groups, 5, tiles, LANES), BF16), ((cases, owned), F32)],
        message, inverse_coarse, field, edge, inverse_rows, total, choice,
        scratch=(VMEM((groups, tiles, LANES), F32),),
    )
    arrived = lax.all_to_all(share, "group", 0, 0, tiled=True)
    total, rounded, edge = call(
        correct_mixed_body,
        [((cases, owned), F32), ((cases, owned), BF16), ((cases, LANES), BF16)],
        arrived, total, *far, basis,
    )
    residual, solution_out = call(
        finish_body,
        [((cases, owned), F32)] * 2,
        rounded, *member_around(rounded, rounded), edge, picks, stiff_rows, own_load, total,
    )
    return (solution_out[None], residual[None])


def solution(mesh):
    placed = (
        P(("group", "member"), None, None),
        P(("group", "member"), None, None),
        P(("group", "member"), None, None),
        P(("group", "member"), None, None),
        P(("group", "member"), None, None),
        P("member", None, "group"),
    )
    return jax.shard_map(
        local,
        mesh=mesh,
        in_specs=placed,
        out_specs=(P(("group", "member"), None, None), P(("group", "member"), None, None)),
        check_vma=False,
    )
```

```python
import jax
import jax.numpy as jnp
from jax import lax
from jax.experimental import pallas as pl
from jax.experimental.pallas import tpu as pltpu
from jax.sharding import PartitionSpec as P


LANES = 128
HALF = 64
CASES = 16
DIGIT = 32
F32 = jnp.float32
BF16 = jnp.bfloat16
VMEM = pltpu.VMEM


def exchanged(shard, axis, first):
    peers = lax.axis_size(axis)
    pairs = [((first + i) % peers, (first + (i ^ 1)) % peers) for i in range(peers)]
    return lax.ppermute(shard, axis, pairs)


def call(body, outs, *args, space=VMEM, scratch=()):
    return pl.pallas_call(
        body,
        out_shape=[jax.ShapeDtypeStruct(shape, dtype) for shape, dtype in outs],
        in_specs=[pl.BlockSpec(memory_space=space)] * len(args),
        out_specs=[pl.BlockSpec(memory_space=VMEM)] * len(outs),
        scratch_shapes=list(scratch),
        compiler_params=pltpu.CompilerParams(vmem_limit_bytes=16 * 2**20),
    )(*args)


def dot_nt(left, right):
    return lax.dot_general(left, right, (((1,), (1,)), ((), ())), preferred_element_type=F32)


def dot_nn(left, right):
    return jnp.dot(left, right, preferred_element_type=F32)


def even(axis):
    return lax.rem(lax.axis_index(axis), 2) == 0


def tall(rows):
    return jnp.concatenate([rows] * (LANES // rows.shape[0]), axis=0)


def lanes(shape):
    return lax.broadcasted_iota(jnp.int32, shape, 1)


def margins(near, next_, pair, other, picks):
    every = dot_nn(jnp.concatenate([near, next_, pair, other], axis=0), picks)
    source = lanes((CASES, picks.shape[1])) // HALF
    by_group = jnp.where(even("group"), 1 - source, source)
    by_member = jnp.where(even("member"), 5 - source, source)
    owner = jnp.where(source < 2, by_group, by_member)
    kept = every[:CASES]
    for d in range(1, 4):
        kept = jnp.where(owner == d, every[d * CASES : (d + 1) * CASES], kept)
    return kept.astype(BF16)


def two_margins(near, next_, picks, axis):
    every = dot_nn(jnp.concatenate([near, next_], axis=0), picks)
    lane = lanes((CASES, LANES))
    swapped = jnp.where(lane < HALF, every[CASES:], every[:CASES])
    straight = jnp.where(lane < HALF, every[:CASES], every[CASES:])
    return jnp.where(even(axis), swapped, straight).astype(BF16)


def one_hot(digits, rows):
    spot = (digits[:, :LANES] * DIGIT + digits[:, LANES:]).astype(jnp.int32)
    choice = lax.broadcasted_iota(jnp.int32, (rows, LANES), 0) == spot
    return jnp.where(choice, 1.0, 0.0).astype(BF16)


def partners(axis, peers):
    me = lax.axis_index(axis)
    upward = even(axis)
    return jnp.where(upward, me + 1, me - 1), lax.rem(jnp.where(upward, me + peers - 1, me + 1), peers)


def begin_body(far_load, far_rows, far_basis, far_inverse, field, picks, basis, for_pair, for_other, for_group, inverse,
               load, rows, sems):
    moves = [
        pltpu.make_async_copy(source, target, sems.at[i])
        for i, (source, target) in enumerate(
            ((far_load, load), (far_rows, rows), (far_basis, basis), (far_inverse, inverse))
        )
    ]
    for move in moves:
        move.start()
    moves[1].wait()
    lists = rows[0]
    nb = basis.shape[1]
    flat = jnp.concatenate([lists[d : d + 1] for d in range(4)], axis=1)
    spots = lax.broadcasted_iota(jnp.int32, picks.shape, 0)
    picks[...] = jnp.where(spots == flat, 1.0, 0.0).astype(BF16)
    moves[0].wait()
    field[...] = load[...].astype(BF16)
    moves[2].wait()
    upward = even("member")
    edge = basis[:, nb - LANES :].astype(F32)
    edge = jnp.where(upward, edge, pltpu.roll(edge, HALF, 1))
    turn = jnp.where(upward, flat[:, LANES:], jnp.concatenate([lists[3:4], lists[2:3]], axis=1))
    around = jnp.where(even("group"), flat[:, :LANES], jnp.concatenate([lists[1:2], lists[0:1]], axis=1))
    tens = (around // DIGIT).astype(F32)
    ones = (around % DIGIT).astype(F32)
    pad = jnp.zeros((1, for_group.shape[1] - 2 * LANES), F32)
    digits = jnp.concatenate([tens, ones, pad], axis=1)
    for_group[...] = jnp.broadcast_to(digits, for_group.shape).astype(BF16)
    high = jnp.broadcast_to((turn // DIGIT).astype(F32), edge.shape)
    low = jnp.broadcast_to((turn % DIGIT).astype(F32), edge.shape)
    parts = jnp.concatenate([edge, high, low], axis=1)
    side = lanes(parts.shape) % LANES >= HALF
    half = parts.shape[0] // 2
    for out, mine in ((for_pair, side), (for_other, jnp.logical_not(side))):
        kept = jnp.where(mine, parts, 0.0).astype(BF16)
        out[...] = jnp.concatenate([kept[:half], kept[half:]], axis=1)
    moves[3].wait()


def restrict_body(v, pair, other, near, next_, picks, basis, block, coef):
    fields = [ref[...].astype(BF16) for ref in (near, next_, pair, other)]
    whole = jnp.concatenate([v[...], margins(*fields, picks[...])], axis=1)
    block[...] = whole
    part = dot_nt(basis[...], tall(whole)).astype(BF16)
    for m in range(coef.shape[0]):
        coef[m] = part


def mixed_body(v, near, next_, pair, other, picks, basis, edge, message):
    value = v[:CASES]
    beside = two_margins(near[:CASES], next_[:CASES], picks[:, :LANES], "group")
    edge[...] = beside
    known = jnp.concatenate([value, beside], axis=1)
    own = dot_nt(basis[:, : known.shape[1]], tall(known))
    width = 3 * LANES
    unfold = lambda ref: jnp.concatenate([ref[:, :width], ref[:, width:]], axis=0)
    first, second = unfold(pair), unfold(other)
    digits = (first[:1, LANES:] + second[:1, LANES:]).astype(F32)
    chosen = dot_nn(value, one_hot(digits, value.shape[1]))
    spread = tall(chosen.astype(BF16))
    to_first = dot_nt(first[:, :LANES], spread)
    to_second = dot_nt(second[:, :LANES], spread)
    head = own.astype(BF16).astype(F32)
    place = lanes(own.shape) // CASES
    out = jnp.concatenate([chosen, pltpu.roll(chosen, HALF, 1)], axis=0)
    out = jnp.where(place == 3, to_second, out)
    out = jnp.where(place == 2, to_first, out)
    out = jnp.where(place == 1, own - head, out)
    out = jnp.where(place == 0, head, out).astype(BF16)
    for m in range(message.shape[0]):
        message[m] = out


def shares_of(every, inverse, share):
    per = LANES // CASES
    lane = lanes(every.shape) // CASES
    tiles = inverse.shape[0] // per
    sums = [None] * tiles
    for q in range(per):
        here = jnp.where(lane == q, every, jnp.zeros_like(every))
        for t in range(tiles):
            term = dot_nn(inverse[per * t + q], here)
            sums[t] = term if sums[t] is None else sums[t] + term
    for t in range(tiles):
        share[:, t, :] = sums[t]


def coarse_body(coef, inverse, share):
    shares_of(coef[...].reshape(-1, LANES), inverse, share)


def coarse_mixed_body(message, inverse, v, edge, inverse_rows, before, choice, basis, out, total, share):
    peers, kdef, _ = message.shape
    source = lax.broadcasted_iota(jnp.int32, (LANES, 3 * LANES), 0)
    target = lanes((LANES, 3 * LANES))
    group = source // CASES
    part = jnp.where(group < 2, 0, group - 1)
    hit = (part == target // LANES) & (source % CASES == target % CASES)
    parts = dot_nn(message[...].reshape(peers * kdef, LANES), jnp.where(hit, 1.0, 0.0).astype(BF16))
    every = []
    for m in range(peers):
        pair = m ^ 1
        other = (m + 1) % peers if m % 2 else (m - 1) % peers
        at = lambda k, j: parts[k * kdef : (k + 1) * kdef, j * LANES : (j + 1) * LANES]
        every.append(at(m, 0) + at(pair, 1) + at(other, 2))
    shares_of(jnp.concatenate(every, axis=0).astype(BF16), inverse, share)
    pair, other = partners("member", peers)
    from_pair = message[pair, :CASES].astype(F32)
    from_other = message[other, CASES:].astype(F32)
    upward = even("member")
    high = jnp.where(upward, from_pair, from_other)
    low = jnp.where(upward, from_other, from_pair)
    left = lanes(high.shape) < HALF
    far = jnp.where(left, pltpu.roll(low, HALF, 1), high).astype(BF16)
    block = jnp.concatenate([v[:CASES], edge[...], far], axis=1)
    value = before[...] + dot_nt(block, inverse_rows[...])
    total[...] = value
    short = share[...].astype(BF16)
    groups = short.shape[0]
    out[:, 0] = short
    out[1:, 1] = short[:-1]
    out[:1, 1] = short[-1:]
    out[:-1, 2] = short[1:]
    out[-1:, 2] = short[:1]
    out[:, 3:] = jnp.zeros((groups, 1) + short.shape[1:], BF16)
    mine = spread_of(share[lax.axis_index("group")], kdef)
    shown = value + dot_nn(mine, basis[:, : value.shape[1]])
    chosen = dot_nn(shown.astype(BF16), choice[...])
    top, low = chosen[: CASES // 2], pltpu.roll(chosen, HALF, 1)[CASES // 2 :]
    side = lanes(top.shape) < HALF
    near, next_ = partners("group", groups)
    rows = short.shape[1]
    slot = jnp.where(even("group"), 1, 2)
    for target, at, kept in (
        (near, slot, jnp.where(side, low, top)),
        (next_, 3 - slot, jnp.where(side, top, low)),
    ):
        kept = kept.astype(BF16)
        out[target, at] = kept[:rows]
        out[target, 3] = kept[rows:]


def prolong_of(arrived, kdef):
    return spread_of(jnp.sum(arrived, axis=0), kdef)


def spread_of(total, kdef):
    tiles = total.shape[0]
    row = lax.broadcasted_iota(jnp.int32, (CASES, LANES), 0)
    lane = lanes((CASES, LANES))
    out = None
    for t in range(tiles):
        spread = jnp.where(lane % CASES == row, total[t : t + 1], 0.0).astype(BF16)
        target = lax.broadcasted_iota(jnp.int32, (LANES, kdef), 0) // CASES + t * (LANES // CASES)
        onto = (target == lanes((LANES, kdef))).astype(BF16)
        term = dot_nn(spread, onto)
        out = term if out is None else out + term
    return out.astype(BF16)


def correct_body(arrived, block, inverse, basis, for_pair, for_other, for_group, total, rounded, pair, other, group):
    value = dot_nt(block[...], inverse[...])
    prolong = prolong_of(arrived[...], basis.shape[0])
    value = value + dot_nn(prolong, basis[:, : total.shape[1]])
    total[...] = value
    short = value.astype(BF16)
    rounded[...] = short
    for out, more in ((pair, for_pair), (other, for_other), (group, for_group)):
        out[:CASES] = short
        out[CASES:] = more[...]


def correct_mixed_body(arrived, before, near, next_, basis, total, rounded, edge):
    kdef = basis.shape[0]
    upward = even("group")
    first, second = partners("group", arrived.shape[0])
    slot = jnp.where(upward, 1, 2)
    take = lambda k, at: jnp.concatenate([arrived[k, at], arrived[k, 3]], axis=0).astype(F32)
    widen = lambda part: jnp.concatenate([part, pltpu.roll(part, HALF, 1)], axis=0)
    left = lanes((CASES, LANES)) < HALF
    known = jnp.where(left, widen(take(second, slot)), widen(take(first, 3 - slot)))
    known = jnp.where(upward, known, pltpu.roll(known, HALF, 1))
    unfold = lambda ref: jnp.concatenate([ref[CASES:, :LANES], ref[CASES:, LANES : 2 * LANES]], axis=0)
    vectors = jnp.where(lanes((kdef, LANES)) < HALF, unfold(next_).astype(F32), unfold(near).astype(F32))
    vectors = jnp.where(upward, vectors, pltpu.roll(vectors, HALF, 1)).astype(BF16)
    me = lax.axis_index("group")
    groups = arrived.shape[0]
    source = lax.broadcasted_iota(jnp.int32, (groups,) + arrived.shape[2:], 0)
    lower, upper = lax.rem(me + groups - 1, groups), lax.rem(me + 1, groups)
    shares = [arrived[:, k].astype(F32) for k in range(3)]
    shares[1] = jnp.where(source == lower, 0.0, shares[1])
    shares[2] = jnp.where(source == upper, 0.0, shares[2])
    prolong = [prolong_of(share, kdef) for share in shares]
    added = jnp.where(left, dot_nn(prolong[1], vectors), dot_nn(prolong[2], vectors))
    edge[...] = (known + added).astype(BF16)
    value = before[...] + dot_nn(prolong[0], basis[:, : total.shape[1]])
    total[...] = value
    rounded[...] = value.astype(BF16)


def residual_body(v, pair, other, near, next_, picks, basis, stiff, load, group, from_pair, from_other, choice):
    edge = margins(near[:CASES], next_[:CASES], pair[:CASES], other[:CASES], picks[...])
    whole = jnp.concatenate([v[...], edge], axis=1)
    value = load[...] - dot_nt(whole, stiff[...])
    from_pair[...] = pair[CASES:]
    from_other[...] = other[CASES:]
    owned = value.shape[1]
    left = lanes((1, 2 * LANES)) % LANES < HALF
    told = lambda ref: ref[CASES : CASES + 1, : 2 * LANES].astype(F32)
    chosen = one_hot(jnp.where(left, told(next_), told(near)), owned)
    choice[...] = chosen
    vectors = dot_nn(basis[:, :owned], chosen).astype(BF16)
    pad = jnp.zeros((CASES, owned - 2 * LANES), BF16)
    group[:CASES] = value.astype(BF16)
    group[CASES:] = jnp.concatenate([vectors[:CASES], vectors[CASES:], pad], axis=1)


def finish_body(v, pair, other, edge, picks, stiff, load, total, out, passed):
    far = two_margins(pair[...], other[...], picks[:, LANES:], "member")
    whole = jnp.concatenate([v[...], edge[...], far], axis=1)
    passed[...] = total[...]
    out[...] = load[...] - dot_nt(whole, stiff[...])


def local(load, stiffness, block_inverse, deflation, margin_rows, coarse_inverse):
    own_load = load[0]
    stiff_rows = stiffness[0]
    inverse_rows = block_inverse[0]
    cases, owned = own_load.shape
    kdef, nb = deflation.shape[1:]
    groups = lax.axis_size("group")
    members = lax.axis_size("member")
    tiles = coarse_inverse.shape[0] * cases // LANES

    def group_around(values):
        near = exchanged(values, "group", 0)
        next_ = exchanged(values, "group", 1)
        return near, next_

    def member_around(for_pair, for_other):
        pair = exchanged(for_pair, "member", 0)
        other = exchanged(for_other, "member", 1)
        return pair, other

    field, picks, basis, for_pair, for_other, for_group, inverse_coarse = call(
        begin_body,
        [((cases, owned), BF16), ((owned, nb - owned), BF16), ((kdef, nb), BF16)]
        + [((kdef // 2, owned), BF16)] * 3
        + [(coarse_inverse.shape, BF16)],
        *(pltpu.with_memory_space_constraint(a, pltpu.HBM) for a in (own_load, margin_rows, deflation[0], coarse_inverse)),
        space=pltpu.HBM,
        scratch=(VMEM((cases, owned), F32), VMEM(margin_rows.shape, jnp.int32), pltpu.SemaphoreType.DMA((4,))),
    )
    near = member_around(own_load, own_load)
    far = group_around(own_load)
    block, coef = call(
        restrict_body,
        [((cases, nb), BF16), ((members, kdef, LANES), BF16)],
        field, *near, *far, picks, basis,
    )
    gathered = lax.all_to_all(coef, "member", 0, 0, tiled=True)
    share_shape = [((groups, tiles, LANES), F32)]
    (share,) = call(coarse_body, share_shape, gathered, inverse_coarse)
    arrived = lax.all_to_all(share, "group", 0, 0, tiled=True)
    total, rounded, for_pair, for_other, for_group = call(
        correct_body,
        [((cases, owned), F32), ((cases, owned), BF16)] + [((cases + kdef // 2, owned), BF16)] * 3,
        arrived, block, inverse_rows, basis, for_pair, for_other, for_group,
    )
    near = member_around(for_pair, for_other)
    field, from_pair, from_other, choice = call(
        residual_body,
        [((cases + kdef // 2, owned), BF16)] + [((kdef // 2, owned), BF16)] * 2 + [((owned, LANES), BF16)],
        rounded, *near, *group_around(for_group), picks, basis, stiff_rows, own_load,
    )

    far = group_around(field)
    edge, message = call(
        mixed_body,
        [((cases, LANES), BF16), ((members, kdef, LANES), BF16)],
        field, *far, from_pair, from_other, picks, basis,
    )
    message = lax.all_to_all(message, "member", 0, 0, tiled=True)
    share, total = call(
        coarse_mixed_body,
        [((groups, 4, tiles, LANES), BF16), ((cases, owned), F32)],
        message, inverse_coarse, field, edge, inverse_rows, total, choice, basis,
        scratch=(VMEM((groups, tiles, LANES), F32),),
    )
    arrived = lax.all_to_all(share, "group", 0, 0, tiled=True)
    total, rounded, edge = call(
        correct_mixed_body,
        [((cases, owned), F32), ((cases, owned), BF16), ((cases, LANES), BF16)],
        arrived, total, *far, basis,
    )
    residual, solution_out = call(
        finish_body,
        [((cases, owned), F32)] * 2,
        rounded, *member_around(rounded, rounded), edge, picks, stiff_rows, own_load, total,
    )
    return (solution_out[None], residual[None])


def solution(mesh):
    placed = (
        P(("group", "member"), None, None),
        P(("group", "member"), None, None),
        P(("group", "member"), None, None),
        P(("group", "member"), None, None),
        P(("group", "member"), None, None),
        P("member", None, "group"),
    )
    return jax.shard_map(
        local,
        mesh=mesh,
        in_specs=placed,
        out_specs=(P(("group", "member"), None, None), P(("group", "member"), None, None)),
        check_vma=False,
    )
```
